128 devices in a mesh: tm: 32 (over x, y, core), col: 4 (over z).
Axes of the slice: x: 4, y: 4, z: 4, core: 2. Of those that a mesh axis runs over, the one named last changes fastest.
Arguments:
- blocks: float32 [128, 512, 512], P('tm', None, 'col'), as said below
- upper: float32 [128, 512, 512], P('tm', None, 'col'), as said below
- arrow: float32 [128, 64, 512], P('tm', None, 'col'), as said below
- tip: float32 [64, 64], replicated, as said below
- rhs: float32 [128, 512], P('tm'), may hold values from -1 to 1
- rhs_fixed: float32 [64], replicated, may hold values from -6 to 6
Outputs:
- solution: float32 [128, 512], P('tm', 'col')
- solution_fixed: float32 [64], replicated
- mean_log_det: float32 [], replicated
The draws below stay inside these ranges and needn't reach their ends.
Inputs may be any that keep to these rules, and one draw needn't show every extreme that they name: blocks[t] is symmetric for every t, and the matrix Q assembled from blocks, upper, arrow and tip is positive definite. `upper`: Q assembled with these couplings is positive definite. `arrow`: Q assembled with these couplings is positive definite. tip is symmetric, and Q assembled with it is positive definite.
All inputs are finite; a program needn't handle non-finite values.
Results may differ from the reference program's by a relative error of at most 0.0003.
Values sent between devices are 32-bit elements; how exact they have to be, the bound alone decides.
No kernel may reach another device: no remote copies, remote signals or barrier semaphores. Data moves between devices by JAX's collectives and lax.ppermute only.
A program may use at most 192 MiB of HBM per device.

```python
import math
import jax
import jax.numpy as jnp
from jax import lax

NODES = 512
EFFECTS = 64
TIMES = 128


def signed_noise(key, shape):
    return jax.random.truncated_normal(key, -4.0, 4.0, shape, jnp.float32)


def log_uniform(key, shape, lowest, highest):
    return jnp.exp(jax.random.uniform(key, shape, jnp.float32, math.log(lowest), math.log(highest)))


def memory_rates(key):
    rate_key = jax.random.fold_in(key, 7005)
    lapse = log_uniform(rate_key, (NODES,), 0.004, 0.06)
    return 1.0 - lapse


def precision_parts(key):
    base_key = jax.random.fold_in(key, 7001)
    mixing_key, scale_key, drift_key = jax.random.split(base_key, 3)
    identity = jnp.eye(NODES, dtype=jnp.float32)
    factors = signed_noise(mixing_key, (TIMES, NODES, NODES))
    spatial = jnp.einsum('tij,tkj->tik', factors, factors, precision=lax.Precision.HIGHEST) / NODES
    spatial = 0.5 * (spatial + jnp.swapaxes(spatial, 1, 2))
    diagonal = log_uniform(scale_key, (TIMES, NODES), 1.0, 2.0)
    spatial = spatial + diagonal[:, :, None] * identity[None]
    rates = memory_rates(key)
    drift_map = rates[None, :, None] * identity[None] + signed_noise(drift_key, (TIMES, NODES, NODES)) * (0.02 / math.sqrt(NODES))
    carried = jnp.einsum('tji,tjk->tik', drift_map, spatial, precision=lax.Precision.HIGHEST)
    return (spatial, drift_map, carried)


def covariate_rows(key):
    return signed_noise(jax.random.fold_in(key, 7003), (TIMES, EFFECTS, NODES)) * (1.5 / math.sqrt(TIMES * NODES))


def draw_blocks(key, part):
    spatial, drift_map, carried = precision_parts(key)
    onward = jnp.einsum('tij,tjk->tik', carried, drift_map, precision=lax.Precision.HIGHEST)
    onward = 0.5 * (onward + jnp.swapaxes(onward, 1, 2))
    onward = jnp.concatenate([onward[1:], jnp.zeros((1, NODES, NODES), jnp.float32)], axis=0)
    nugget_key = jax.random.fold_in(key, 7002)
    nugget = log_uniform(nugget_key, (TIMES, NODES), 0.002, 0.006)
    return spatial + onward + nugget[:, :, None] * jnp.eye(NODES, dtype=jnp.float32)[None]


def draw_upper(key, part):
    spatial, drift_map, carried = precision_parts(key)
    return -carried


def draw_arrow(key, part):
    spatial, drift_map, carried = precision_parts(key)
    covariates = covariate_rows(key)
    direct = jnp.einsum('tej,tjk->tek', covariates, spatial, precision=lax.Precision.HIGHEST)
    lagged = jnp.einsum('tej,tij->tei', covariates, carried, precision=lax.Precision.HIGHEST)
    lagged = jnp.concatenate([lagged[1:], jnp.zeros((1, EFFECTS, NODES), jnp.float32)], axis=0)
    return lagged - direct


def draw_tip(key, part):
    spatial, drift_map, carried = precision_parts(key)
    covariates = covariate_rows(key)
    weighted = jnp.einsum('tej,tjk->tek', covariates, spatial, precision=lax.Precision.HIGHEST)
    loading = jnp.einsum('tek,tfk->ef', weighted, covariates, precision=lax.Precision.HIGHEST)
    loading = 0.5 * (loading + loading.T)
    matrix_key, scale_key = jax.random.split(jax.random.fold_in(key, 404))
    mixing = signed_noise(matrix_key, (EFFECTS, EFFECTS))
    product = jnp.dot(mixing, mixing.T, precision=lax.Precision.HIGHEST) / EFFECTS
    product = 0.5 * (product + product.T)
    diagonal = log_uniform(scale_key, (EFFECTS,), 2.0, 4.0)
    return product + jnp.diag(diagonal) + loading


def draw_rhs(key, part):
    noise_key = jax.random.fold_in(jax.random.fold_in(key, 7004), 0)
    rough_part = signed_noise(noise_key, (TIMES, NODES)) * 0.25
    return rough_part


def centred(stream_key, dims, scale, reach, kind=jnp.bfloat16):
    return jnp.clip(scale * jax.random.normal(stream_key, dims, jnp.float32), -reach, reach).astype(kind)


def setup_inputs(seed: int = 0) -> dict:
    streams_of = jax.random.split(jax.random.key(seed), 7)
    return {
        "blocks": draw_blocks(jax.random.fold_in(streams_of[6], 71), 0),
        "upper": draw_upper(jax.random.fold_in(streams_of[6], 71), 0),
        "arrow": draw_arrow(jax.random.fold_in(streams_of[6], 71), 0),
        "tip": draw_tip(jax.random.fold_in(streams_of[6], 71), 0),
        "rhs": draw_rhs(jax.random.fold_in(streams_of[6], 71), 0),
        "rhs_fixed": centred(streams_of[5], (EFFECTS,), 1.0, 6.0, jnp.float32),
    }


def lower_solve(factor, right_side):
    return lax.linalg.triangular_solve(factor, right_side, left_side=True, lower=True)

def upper_solve(factor, right_side):
    return lax.linalg.triangular_solve(factor, right_side, left_side=True, lower=True, transpose_a=True)

def cross_product(first_operand, second_operand):
    return lax.dot_general(first_operand.astype(jnp.float32), second_operand.astype(jnp.float32), (((0,), (0,)), ((), ())), precision=lax.Precision.HIGHEST, preferred_element_type=jnp.float32)

def apply_matrix(matrix, vector):
    return jnp.dot(matrix.astype(jnp.float32), vector.astype(jnp.float32), precision=lax.Precision.HIGHEST, preferred_element_type=jnp.float32)

def reference(blocks, upper, arrow, tip, rhs, rhs_fixed):
    step_ids = jnp.arange(TIMES, dtype=jnp.int32)

    def forward(carry, inputs):
        factor_prev, side_prev, right_prev, tip_sum, fixed_sum, log_sum = carry
        block, coupling, side_block, right_block, step_id = inputs
        coupled = lower_solve(factor_prev, coupling) * (step_id > 0).astype(jnp.float32)
        factor = jnp.linalg.cholesky(block - cross_product(coupled, coupled))
        side_solved = lower_solve(factor, side_block.T - cross_product(coupled, side_prev))
        right_solved = lower_solve(factor, (right_block - cross_product(coupled, right_prev))[:, None])[:, 0]
        tip_sum = tip_sum + cross_product(side_solved, side_solved)
        fixed_sum = fixed_sum + cross_product(side_solved, right_solved)
        log_sum = log_sum + 2.0 * jnp.sum(jnp.log(jnp.diagonal(factor)))
        return ((factor, side_solved, right_solved, tip_sum, fixed_sum, log_sum), (factor, coupled, side_solved, right_solved))
    initial = (jnp.eye(NODES, dtype=jnp.float32), jnp.zeros((NODES, EFFECTS), jnp.float32), jnp.zeros((NODES,), jnp.float32), jnp.zeros((EFFECTS, EFFECTS), jnp.float32), jnp.zeros((EFFECTS,), jnp.float32), jnp.zeros((), jnp.float32))
    final_carry, stacked = lax.scan(forward, initial, (blocks, upper, arrow, rhs, step_ids))
    tip_sum, fixed_sum, log_sum = (final_carry[3], final_carry[4], final_carry[5])
    factors, couplings, sides, rights = stacked
    fixed_factor = jnp.linalg.cholesky(tip - tip_sum)
    fixed_solved = lower_solve(fixed_factor, (rhs_fixed - fixed_sum)[:, None])
    solution_fixed = upper_solve(fixed_factor, fixed_solved)[:, 0]
    log_total = log_sum + 2.0 * jnp.sum(jnp.log(jnp.diagonal(fixed_factor)))
    next_couplings = jnp.concatenate([couplings[1:], jnp.zeros((1, NODES, NODES), jnp.float32)], axis=0)

    def backward(following, inputs):
        factor, coupling_next, side_solved, right_solved = inputs
        terms = apply_matrix(coupling_next, following) + apply_matrix(side_solved, solution_fixed)
        value = upper_solve(factor, (right_solved - terms)[:, None])[:, 0]
        return (value, value)
    last_value, solution = lax.scan(backward, jnp.zeros((NODES,), jnp.float32), (factors, next_couplings, sides, rights), reverse=True)
    return (solution, solution_fixed, log_total / (TIMES * NODES + EFFECTS))
```

```python
import jax
import jax.numpy as jnp
from jax import lax
from jax.experimental import pallas as pl
from jax.experimental.pallas import tpu as pltpu
from jax.sharding import PartitionSpec as P

AXES = ("tm", "col")
F32 = jnp.float32
TILE = 128
HALF = 256
NODES = 512


def mm(a, b):
    return lax.dot_general(
        a, b, (((1,), (0,)), ((), ())), precision=lax.Precision.HIGHEST, preferred_element_type=F32
    )


def mtm(a, b):
    return lax.dot_general(
        a, b, (((0,), (0,)), ((), ())), precision=lax.Precision.HIGHEST, preferred_element_type=F32
    )


def lane_splat(x, j):
    return jnp.broadcast_to(x[:, j : j + 1], (8, TILE))


def row_splat(x, i):
    return jnp.broadcast_to(x[i : i + 1, :], (8, TILE))


def factor_tile(tile, inv_ref, size):
    groups = size // 8
    a = [tile[8 * g : 8 * g + 8, :] for g in range(groups)]
    row = lax.broadcasted_iota(jnp.int32, (8, TILE), 0)
    lane = lax.broadcasted_iota(jnp.int32, (8, TILE), 1)
    inv = [jnp.where(lane == row + 8 * g, 1.0, 0.0).astype(F32) for g in range(groups)]
    pivots = jnp.ones((8, TILE), F32)
    for g0 in range(groups):
        top, side = a[g0], inv[g0]
        cols = [lane_splat(top, 8 * g0 + i) for i in range(8)]
        rows = [row_splat(top, i) for i in range(8)]
        side_rows = [row_splat(side, i) for i in range(8)]
        p = [[row_splat(cols[c], i) for c in range(i + 1)] for i in range(8)]
        low = [[None] * 8 for _ in range(8)]
        scale = []
        for c in range(8):
            r = lax.rsqrt(p[c][c])
            scale.append(r)
            pivots = jnp.where((row == c) & (lane == g0), p[c][c], pivots)
            for i in range(c + 1, 8):
                low[i][c] = p[i][c] * r
            for i in range(c + 1, 8):
                for k in range(c + 1, i + 1):
                    p[i][k] = p[i][k] - low[i][c] * low[k][c]
        u, v = [], []
        for i in range(8):
            x, y = rows[i], side_rows[i]
            for c in range(i):
                x = x - low[i][c] * u[c]
                y = y - low[i][c] * v[c]
            u.append(x * scale[i])
            v.append(y * scale[i])
        for g in range(g0 + 1, groups):
            e = []
            for i in range(8):
                x = lane_splat(a[g], 8 * g0 + i)
                for c in range(i):
                    x = x - low[i][c] * e[c]
                e.append(x * scale[i])
            for i in range(8):
                a[g] = a[g] - e[i] * u[i]
                inv[g] = inv[g] - e[i] * v[i]
        done = side
        for i in range(8):
            done = jnp.where(row == i, v[i], done)
        inv[g0] = done
    for g in range(groups):
        inv_ref[8 * g : 8 * g + 8, :] = inv[g]
    return pivots


def factor_body(s, inv, ma, mb, u):
    def body(k, logs):
        o = pl.multiple_of(k * TILE, TILE)
        pivots = factor_tile(s[pl.ds(o, TILE), pl.ds(o, TILE)], inv, TILE)
        for half, m in ((0, ma), (1, mb)):
            b0, b1, b2 = half * HALF, half * HALF + TILE, half * HALF + HALF

            @pl.when(k == 2 * half)
            def _():
                first = inv[...]
                panel = mm(first, s[b0:b1, b1:b2])
                s[b1:b2, b1:b2] = s[b1:b2, b1:b2] - mtm(panel, panel)
                m[0:TILE, 0:TILE] = first
                m[0:TILE, TILE:HALF] = jnp.zeros((TILE, TILE), F32)
                m[TILE:HALF, 0:TILE] = mtm(panel, first)

            @pl.when(k == 2 * half + 1)
            def _():
                second = inv[...]
                m[TILE:HALF, TILE:HALF] = second
                m[TILE:HALF, 0:TILE] = -mm(second, m[TILE:HALF, 0:TILE])
                if half == 0:
                    panel = mm(ma[...], s[0:HALF, HALF:NODES])
                    u[...] = panel
                    s[HALF:NODES, HALF:NODES] = s[HALF:NODES, HALF:NODES] - mtm(panel, panel)

        return logs + jnp.log(pivots)

    return lax.fori_loop(0, 4, body, jnp.zeros((8, TILE), F32))


def factor_first_kernel(q, ma, mb, u, logs, s, inv):
    s[...] = q[...]
    logs[...] = factor_body(s, inv, ma, mb, u)


def factor_next_kernel(q, from_left, from_right, ma, mb, u, logs, q_new, s, inv):
    value = q[...] - from_left[...] - from_right[...]
    s[...] = value
    q_new[...] = value
    logs[...] = factor_body(s, inv, ma, mb, u)


def solve_into(ma, mb, u, top, bottom, out):
    first = mm(ma[...], top)
    out[0:HALF, :] = first
    out[HALF:NODES, :] = mm(mb[...], bottom - mtm(u[...], first))


def packed_products(w, ws, out, corner):
    whole, edge = w[...], ws[...]
    out[0:HALF, :] = mtm(w[:, 0:HALF], whole)
    out[HALF:NODES, HALF:NODES] = mtm(w[:, HALF:NODES], w[:, HALF:NODES])
    crossed = mtm(whole, edge)
    out[HALF:NODES, 0:TILE] = crossed[0:HALF]
    out[HALF:NODES, TILE:HALF] = crossed[HALF:NODES]
    out[TILE:HALF, 0:TILE] = corner


def corner_sums(q, ws, logs):
    row = lax.broadcasted_iota(jnp.int32, (TILE, TILE), 0)
    lane = lax.broadcasted_iota(jnp.int32, (TILE, TILE), 1)
    log_sum = jnp.sum(logs[...])
    sums = mtm(ws[...], ws[...]) - q[TILE:HALF, 0:TILE]
    return sums + jnp.where((row == 65) & (lane == 65), log_sum, 0.0)


def eliminate_kernel(ma, mb, u, logs, q, low, high, wl, wh, ws, left, right):
    solve_into(ma, mb, u, q[HALF:NODES, 0:TILE], q[HALF:NODES, TILE:HALF], ws)
    solve_into(ma, mb, u, low[0:HALF, :], low[HALF:NODES, :], wl)
    packed_products(wl, ws, left, jnp.zeros((TILE, TILE), F32))
    solve_into(ma, mb, u, high[0:HALF, :], high[HALF:NODES, :], wh)
    packed_products(wh, ws, right, corner_sums(q, ws, logs))


def couple_kernel(odd, wl, wh, out):
    @pl.when(odd[0] == 0)
    def _():
        out[...] = -mtm(wh[...], wl[...])

    @pl.when(odd[0] != 0)
    def _():
        out[...] = -mtm(wl[...], wh[...])


def back_solve(ma, mb, u, z_top, z_bottom):
    x_bottom = jnp.sum(mb[...] * z_bottom, axis=0, keepdims=True)
    z_top = z_top - jnp.sum(u[...] * x_bottom, axis=1, keepdims=True)
    x_top = jnp.sum(ma[...] * z_top, axis=0, keepdims=True)
    return x_top, x_bottom


def root_kernel(total, ma, mb, u, logs, q, tip, fixed, out, ws, inv):
    solve_into(ma, mb, u, q[HALF:NODES, 0:TILE], q[HALF:NODES, TILE:HALF], ws)
    sums = corner_sums(q, ws, logs)
    row = lax.broadcasted_iota(jnp.int32, (TILE, TILE), 0)
    lane = lax.broadcasted_iota(jnp.int32, (TILE, TILE), 1)
    inv[...] = tip[...] - jnp.where((row < 64) & (lane < 64), sums, 0.0)
    pivots = factor_tile(inv[0:64, :], inv, 64)
    m = inv[0:64, :]
    rest = fixed[...] - sums[64:65, :]
    z = jnp.sum(m * rest, axis=1, keepdims=True)
    x_fixed = jnp.sum(m * z, axis=0, keepdims=True)
    lane1 = lax.broadcasted_iota(jnp.int32, (1, TILE), 1)
    x_fixed = jnp.where(lane1 < 64, x_fixed, 0.0)
    log_total = jnp.sum(jnp.where((row == 65) & (lane == 65), sums, 0.0)) + jnp.sum(jnp.log(pivots))
    weights = jnp.where(lane1 == 64, 1.0, -x_fixed)
    z = jnp.sum(ws[...] * weights, axis=1, keepdims=True)
    x_top, x_bottom = back_solve(ma, mb, u, z[0:HALF], z[HALF:NODES])
    out[:, 0:HALF] = x_top
    out[:, HALF:NODES] = x_bottom
    out[:, NODES : NODES + TILE] = jnp.where(lane1 == 64, log_total / total, x_fixed)


def back_kernel(leaving, from_left, from_right, own, ma, mb, u, wl, wh, ws, out):
    lane1 = lax.broadcasted_iota(jnp.int32, (1, TILE), 1)
    extra = from_right[:, NODES : NODES + TILE]
    weights = jnp.where(lane1 == 64, 1.0, jnp.where(lane1 < 64, -extra, 0.0))
    z = (
        jnp.sum(ws[...] * weights, axis=1, keepdims=True)
        - jnp.sum(wl[...] * from_left[:, 0:NODES], axis=1, keepdims=True)
        - jnp.sum(wh[...] * from_right[:, 0:NODES], axis=1, keepdims=True)
    )
    x_top, x_bottom = back_solve(ma, mb, u, z[0:HALF], z[HALF:NODES])
    mine = leaving[0] != 0
    out[:, 0:HALF] = jnp.where(mine, x_top, own[:, 0:HALF])
    out[:, HALF:NODES] = jnp.where(mine, x_bottom, own[:, HALF:NODES])
    out[:, NODES : NODES + TILE] = jnp.where(mine, extra, own[:, NODES : NODES + TILE])


def shape(*dims):
    return jax.ShapeDtypeStruct(dims, F32)


def call(kernel, ins, outs, scratch=(), scalars=0, flops=0):
    smem = pl.BlockSpec(memory_space=pltpu.SMEM)
    vmem = pl.BlockSpec(memory_space=pltpu.VMEM)
    moved = 4 * sum(a.size for a in ins) + 4 * sum(o.size for o in outs)
    return pl.pallas_call(
        kernel,
        out_shape=tuple(outs),
        in_specs=[smem] * scalars + [vmem] * (len(ins) - scalars),
        out_specs=tuple([vmem] * len(outs)),
        scratch_shapes=[pltpu.VMEM(dims, F32) for dims in scratch],
        cost_estimate=pl.CostEstimate(flops=flops, bytes_accessed=moved, transcendentals=0),
    )(*ins)


FACTORS = (shape(HALF, HALF), shape(HALF, HALF), shape(HALF, HALF), shape(8, TILE))
WORK = ((NODES, NODES), (TILE, TILE))


def moved(x, pairs):
    return lax.ppermute(x, AXES, pairs)


def per_device(blocks, upper, arrow, tip, rhs, rhs_fixed):
    node_count = blocks.shape[1]
    effects = tip.shape[0]
    cols = lax.axis_size("col")
    count = lax.axis_size("tm") * cols
    col = lax.axis_index("col")
    t = lax.axis_index("tm") * cols + col
    take = lambda x: lax.all_to_all(x, "col", split_axis=0, concat_axis=2, tiled=True)[0]
    diagonal = take(blocks)
    coupling = take(upper)
    side = take(arrow)
    own_rhs = lax.dynamic_slice_in_dim(rhs, col, 1, 0)
    ma, mb, u, logs = call(factor_first_kernel, (diagonal,), FACTORS, WORK, flops=4 * 10**9)
    high = moved(coupling, [(i + 1, i) for i in range(0, count, 2)])
    low = coupling.T * (t > 0).astype(F32)
    edge = jnp.concatenate(
        [side, own_rhs, jnp.zeros((TILE - effects - 1, node_count), F32)], axis=0
    ).T
    packed = jnp.concatenate([edge[0:HALF], edge[HALF:NODES]], axis=1)
    q = diagonal.at[HALF:NODES, 0:HALF].set(packed)
    q = q.at[TILE:HALF, 0:TILE].set(0.0)
    kept = []
    level = 0
    while (1 << level) < count:
        s = 1 << level
        leaving = [(2 * k + 1) * s - 1 for k in range(count // (2 * s))]
        products = (shape(NODES, NODES), shape(NODES, NODES), shape(NODES, TILE)) + (
            shape(NODES, NODES),
        ) * 2
        wl, wh, ws, left, right = call(
            eliminate_kernel, (ma, mb, u, logs, q, low, high), products, flops=6 * 10**9
        )
        kept.append((ma, mb, u, wl, wh, ws))
        got_left = moved(right, [(i, i + s) for i in leaving])
        got_right = moved(left, [(i, i - s) for i in leaving if i >= s])
        if 2 * s < count:
            odd = (((t + 1) // (2 * s)) % 2).astype(jnp.int32).reshape(1)
            (new,) = call(couple_kernel, (odd, wl, wh), (shape(NODES, NODES),), scalars=1, flops=10**9)
            new, got_left, got_right = lax.optimization_barrier((new, got_left, got_right))
            low = moved(new, [(i, i + s) for i in leaving[0::2]])
            high = moved(new, [(i, i - s) for i in leaving[1::2]])
        ma, mb, u, logs, q = call(
            factor_next_kernel,
            (q, got_left, got_right),
            FACTORS + (shape(NODES, NODES),),
            WORK,
            flops=4 * 10**9,
        )
        level += 1
    whole_tip = jnp.eye(TILE, dtype=F32).at[0:effects, 0:effects].set(tip)
    whole_fixed = jnp.pad(rhs_fixed, (0, TILE - effects)).reshape(1, TILE)
    total = float(count * node_count + effects)
    (state,) = call(
        lambda *refs: root_kernel(total, *refs),
        (ma, mb, u, logs, q, whole_tip, whole_fixed),
        (shape(1, NODES + TILE),),
        ((NODES, TILE), (TILE, TILE)),
        flops=10**8,
    )
    for level in reversed(range(len(kept))):
        s = 1 << level
        leaving = [(2 * k + 1) * s - 1 for k in range(count // (2 * s))]
        from_left = moved(state, [(i - s, i) for i in leaving if i >= s])
        from_right = moved(state, [(i + s, i) for i in leaving])
        mine = ((t + 1) % (2 * s) == s).astype(jnp.int32).reshape(1)
        (state,) = call(
            back_kernel,
            (mine, from_left, from_right, state) + kept[level],
            (shape(1, NODES + TILE),),
            scalars=1,
            flops=10**7,
        )
    solution = lax.all_to_all(state[:, 0:NODES], "col", split_axis=1, concat_axis=0, tiled=True)
    return (solution, state[0, NODES : NODES + effects], state[0, NODES + 64])


def solution(mesh):
    placed = (
        P("tm", None, "col"),
        P("tm", None, "col"),
        P("tm", None, "col"),
        P(),
        P("tm", None),
        P(),
    )
    return jax.shard_map(
        per_device,
        mesh=mesh,
        in_specs=placed,
        out_specs=(P("tm", "col"), P(), P()),
        check_vma=False,
    )
```

```python
import jax
import jax.numpy as jnp
from jax import lax
from jax.experimental import pallas as pl
from jax.experimental.pallas import tpu as pltpu
from jax.sharding import PartitionSpec as P

AXES = ("tm", "col")
F32 = jnp.float32
TILE = 128
HALF = 256
NODES = 512
EFFECTS = 64


def mm(a, b):
    return lax.dot_general(
        a, b, (((1,), (0,)), ((), ())), precision=lax.Precision.HIGHEST, preferred_element_type=F32
    )


def mtm(a, b):
    return lax.dot_general(
        a, b, (((0,), (0,)), ((), ())), precision=lax.Precision.HIGHEST, preferred_element_type=F32
    )


def lane_splat(x, j):
    return jnp.broadcast_to(x[:, j : j + 1], (8, TILE))


def row_splat(x, i):
    return jnp.broadcast_to(x[i : i + 1, :], (8, TILE))


def factor_tile(tile, inv_ref, size):
    groups = size // 8
    a = [tile[8 * g : 8 * g + 8, :] for g in range(groups)]
    row = lax.broadcasted_iota(jnp.int32, (8, TILE), 0)
    lane = lax.broadcasted_iota(jnp.int32, (8, TILE), 1)
    inv = [jnp.where(lane == row + 8 * g, 1.0, 0.0).astype(F32) for g in range(groups)]
    pivots = jnp.ones((8, TILE), F32)
    for g0 in range(groups):
        top, side = a[g0], inv[g0]
        cols = [lane_splat(top, 8 * g0 + i) for i in range(8)]
        rows = [row_splat(top, i) for i in range(8)]
        side_rows = [row_splat(side, i) for i in range(8)]
        p = [[row_splat(cols[c], i) for c in range(i + 1)] for i in range(8)]
        low = [[None] * 8 for _ in range(8)]
        scale = []
        for c in range(8):
            r = lax.rsqrt(p[c][c])
            scale.append(r)
            pivots = jnp.where((row == c) & (lane == g0), p[c][c], pivots)
            for i in range(c + 1, 8):
                low[i][c] = p[i][c] * r
            for i in range(c + 1, 8):
                for k in range(c + 1, i + 1):
                    p[i][k] = p[i][k] - low[i][c] * low[k][c]
        u, v = [], []
        for i in range(8):
            x, y = rows[i], side_rows[i]
            for c in range(i):
                x = x - low[i][c] * u[c]
                y = y - low[i][c] * v[c]
            u.append(x * scale[i])
            v.append(y * scale[i])
        for g in range(g0 + 1, groups):
            e = []
            for i in range(8):
                x = lane_splat(a[g], 8 * g0 + i)
                for c in range(i):
                    x = x - low[i][c] * e[c]
                e.append(x * scale[i])
            for i in range(8):
                a[g] = a[g] - e[i] * u[i]
                inv[g] = inv[g] - e[i] * v[i]
        done = side
        for i in range(8):
            done = jnp.where(row == i, v[i], done)
        inv[g0] = done
    for g in range(groups):
        inv_ref[8 * g : 8 * g + 8, :] = inv[g]
    return pivots


def factor_body(s, inv, ma, mb, u):
    def body(k, logs):
        o = pl.multiple_of(k * TILE, TILE)
        pivots = factor_tile(s[pl.ds(o, TILE), pl.ds(o, TILE)], inv, TILE)
        for half, m in ((0, ma), (1, mb)):
            b0, b1, b2 = half * HALF, half * HALF + TILE, half * HALF + HALF

            @pl.when(k == 2 * half)
            def _():
                first = inv[...]
                panel = mm(first, s[b0:b1, b1:b2])
                s[b1:b2, b1:b2] = s[b1:b2, b1:b2] - mtm(panel, panel)
                m[0:TILE, 0:TILE] = first
                m[0:TILE, TILE:HALF] = jnp.zeros((TILE, TILE), F32)
                m[TILE:HALF, 0:TILE] = mtm(panel, first)

            @pl.when(k == 2 * half + 1)
            def _():
                second = inv[...]
                m[TILE:HALF, TILE:HALF] = second
                m[TILE:HALF, 0:TILE] = -mm(second, m[TILE:HALF, 0:TILE])
                if half == 0:
                    panel = mm(ma[...], s[0:HALF, HALF:NODES])
                    u[...] = panel
                    s[HALF:NODES, HALF:NODES] = s[HALF:NODES, HALF:NODES] - mtm(panel, panel)

        return logs + jnp.log(pivots)

    return lax.fori_loop(0, 4, body, jnp.zeros((8, TILE), F32))


def factor_first_kernel(place, own, one, two, three, rhs, ma, mb, u, logs, q_new, s, inv):
    col, pos = place[0], place[1]
    right = rhs[pl.ds(pos, 1), :]
    for back, ref in enumerate((own, one, two, three)):
        source = lax.rem(col - back + 4, 4)
        o = pl.multiple_of(source * TILE, TILE)
        s[:, pl.ds(o, TILE)] = ref[0:NODES, :]
    q_new[...] = s[...]
    q_new[TILE:HALF, 0:TILE] = jnp.zeros((TILE, TILE), F32)
    row = lax.broadcasted_iota(jnp.int32, (TILE - EFFECTS, TILE), 0)
    for back, ref in enumerate((own, one, two, three)):
        source = lax.rem(col - back + 4, 4)
        part = jnp.zeros((1, TILE), F32)
        for k in range(4):
            part = jnp.where(source == k, right[:, k * TILE : (k + 1) * TILE], part)
        rest = jnp.where(row == 0, jnp.broadcast_to(part, row.shape), 0.0)
        edge = jnp.concatenate([ref[NODES : NODES + EFFECTS, :], rest], axis=0).T
        o0 = pl.multiple_of(HALF + lax.rem(source, 2) * TILE, TILE)
        o1 = pl.multiple_of((source // 2) * TILE, TILE)
        q_new[pl.ds(o0, TILE), pl.ds(o1, TILE)] = edge
    logs[...] = factor_body(s, inv, ma, mb, u)


def couple_first_kernel(place, own, one, two, three, low, high):
    col, keep = place[0], place[2]
    for back, ref in enumerate((own, one, two, three)):
        source = lax.rem(col - back + 4, 4)
        o = pl.multiple_of(source * TILE, TILE)
        high[:, pl.ds(o, TILE)] = ref[1]
        low[pl.ds(o, TILE), :] = jnp.where(keep > 0, ref[0].T, 0.0)


def factor_next_kernel(count, *refs):
    parts, (ma, mb, u, logs, q_new, s, inv) = refs[:count], refs[count:]
    value = parts[0][...]
    for part in parts[1:]:
        value = value - part[...]
    s[...] = value
    q_new[...] = value
    logs[...] = factor_body(s, inv, ma, mb, u)


def solve_into(ma, mb, u, top, bottom, out):
    first = mm(ma[...], top)
    out[0:HALF, :] = first
    out[HALF:NODES, :] = mm(mb[...], bottom - mtm(u[...], first))


def packed_products(w, ws, out, corner):
    whole, edge = w[...], ws[...]
    out[0:HALF, :] = mtm(w[:, 0:HALF], whole)
    out[HALF:NODES, HALF:NODES] = mtm(w[:, HALF:NODES], w[:, HALF:NODES])
    crossed = mtm(whole, edge)
    out[HALF:NODES, 0:TILE] = crossed[0:HALF]
    out[HALF:NODES, TILE:HALF] = crossed[HALF:NODES]
    out[TILE:HALF, 0:TILE] = corner


def corner_sums(q, ws, logs):
    row = lax.broadcasted_iota(jnp.int32, (TILE, TILE), 0)
    lane = lax.broadcasted_iota(jnp.int32, (TILE, TILE), 1)
    log_sum = jnp.sum(logs[...])
    sums = mtm(ws[...], ws[...]) - q[TILE:HALF, 0:TILE]
    return sums + jnp.where((row == 65) & (lane == 65), log_sum, 0.0)


def near_kernel(odd, ma, mb, u, logs, q, low, high, wn, ws, out):
    flag = odd[0] != 0
    pick = lambda rows: jnp.where(flag, low[rows, :], high[rows, :])
    solve_into(ma, mb, u, q[HALF:NODES, 0:TILE], q[HALF:NODES, TILE:HALF], ws)
    solve_into(ma, mb, u, pick(slice(0, HALF)), pick(slice(HALF, NODES)), wn)
    packed_products(wn, ws, out, jnp.where(flag, 0.0, corner_sums(q, ws, logs)))


def far_kernel(count, odd, ma, mb, u, logs, low, high, wn, ws, *refs):
    parts, outs = refs[: 1 + count], refs[1 + count :]
    wf, new, out = outs[:3]
    q = parts[0]
    flag = odd[0] != 0
    pick = lambda rows: jnp.where(flag, high[rows, :], low[rows, :])
    solve_into(ma, mb, u, pick(slice(0, HALF)), pick(slice(HALF, NODES)), wf)
    new[...] = -mtm(wn[...], wf[...])
    packed_products(wf, ws, out, jnp.where(flag, corner_sums(q, ws, logs), 0.0))
    if count:
        value = q[...]
        for part in parts[1:]:
            value = value - part[...]
        outs[3][...] = value


def back_solve(ma, mb, u, z_top, z_bottom):
    x_bottom = jnp.sum(mb[...] * z_bottom, axis=0, keepdims=True)
    z_top = z_top - jnp.sum(u[...] * x_bottom, axis=1, keepdims=True)
    x_top = jnp.sum(ma[...] * z_top, axis=0, keepdims=True)
    return x_top, x_bottom


def root_kernel(total, ma, mb, u, logs, q, tip, fixed, out, ws, inv):
    solve_into(ma, mb, u, q[HALF:NODES, 0:TILE], q[HALF:NODES, TILE:HALF], ws)
    sums = corner_sums(q, ws, logs)
    row = lax.broadcasted_iota(jnp.int32, (TILE, TILE), 0)
    lane = lax.broadcasted_iota(jnp.int32, (TILE, TILE), 1)
    inv[...] = tip[...] - jnp.where((row < 64) & (lane < 64), sums, 0.0)
    pivots = factor_tile(inv[0:64, :], inv, 64)
    m = inv[0:64, :]
    rest = fixed[...] - sums[64:65, :]
    z = jnp.sum(m * rest, axis=1, keepdims=True)
    x_fixed = jnp.sum(m * z, axis=0, keepdims=True)
    lane1 = lax.broadcasted_iota(jnp.int32, (1, TILE), 1)
    x_fixed = jnp.where(lane1 < 64, x_fixed, 0.0)
    log_total = jnp.sum(jnp.where((row == 65) & (lane == 65), sums, 0.0)) + jnp.sum(jnp.log(pivots))
    weights = jnp.where(lane1 == 64, 1.0, -x_fixed)
    z = jnp.sum(ws[...] * weights, axis=1, keepdims=True)
    x_top, x_bottom = back_solve(ma, mb, u, z[0:HALF], z[HALF:NODES])
    out[:, 0:HALF] = x_top
    out[:, HALF:NODES] = x_bottom
    out[:, NODES : NODES + TILE] = jnp.where(lane1 == 64, log_total / total, x_fixed)


def back_kernel(flags, from_left, from_right, own, ma, mb, u, wn, wf, ws, out):
    lane1 = lax.broadcasted_iota(jnp.int32, (1, TILE), 1)
    extra = from_right[:, NODES : NODES + TILE]
    weights = jnp.where(lane1 == 64, 1.0, jnp.where(lane1 < 64, -extra, 0.0))
    odd = flags[1] != 0
    x_left, x_right = from_left[:, 0:NODES], from_right[:, 0:NODES]
    x_near, x_far = jnp.where(odd, x_left, x_right), jnp.where(odd, x_right, x_left)
    z = jnp.sum(ws[...] * weights, axis=1, keepdims=True) - jnp.sum(
        wn[...] * x_near + wf[...] * x_far, axis=1, keepdims=True
    )
    x_top, x_bottom = back_solve(ma, mb, u, z[0:HALF], z[HALF:NODES])
    mine = flags[0] != 0
    out[:, 0:HALF] = jnp.where(mine, x_top, own[:, 0:HALF])
    out[:, HALF:NODES] = jnp.where(mine, x_bottom, own[:, HALF:NODES])
    out[:, NODES : NODES + TILE] = jnp.where(mine, extra, own[:, NODES : NODES + TILE])


def shape(*dims):
    return jax.ShapeDtypeStruct(dims, F32)


def call(kernel, ins, outs, scratch=(), scalars=0, flops=0):
    smem = pl.BlockSpec(memory_space=pltpu.SMEM)
    vmem = pl.BlockSpec(memory_space=pltpu.VMEM)
    moved = 4 * sum(a.size for a in ins) + 4 * sum(o.size for o in outs)
    return pl.pallas_call(
        kernel,
        out_shape=tuple(outs),
        in_specs=[smem] * scalars + [vmem] * (len(ins) - scalars),
        out_specs=tuple([vmem] * len(outs)),
        scratch_shapes=[pltpu.VMEM(dims, F32) for dims in scratch],
        cost_estimate=pl.CostEstimate(flops=flops, bytes_accessed=moved, transcendentals=0),
    )(*ins)


FACTORS = (shape(HALF, HALF), shape(HALF, HALF), shape(HALF, HALF), shape(8, TILE))
WORK = ((NODES, NODES), (TILE, TILE))


def device_of(t):
    return (t // 4) * 4 + (t % 4 + 2 * ((t // 4) % 2)) % 4


def moved(x, pairs):
    return lax.ppermute(x, AXES, [(device_of(i), device_of(j)) for i, j in pairs])


def per_device(blocks, upper, arrow, tip, rhs, rhs_fixed):
    node_count = blocks.shape[1]
    effects = tip.shape[0]
    cols = 4
    count = lax.axis_size("tm") * cols
    col, shift = lax.axis_index("col"), 2 * (lax.axis_index("tm") % 2)
    pos = (col + shift) % cols
    t = lax.axis_index("tm") * cols + pos
    place = jnp.stack([col, pos, (t > 0).astype(jnp.int32)]).astype(jnp.int32)

    def diagonal_for(p):
        return jnp.concatenate(
            [
                lax.dynamic_index_in_dim(blocks, p, 0, keepdims=False),
                lax.dynamic_index_in_dim(arrow, p, 0, keepdims=False),
            ],
            axis=0,
        )

    got, wanted = [diagonal_for(pos)], [lax.dynamic_slice_in_dim(upper, pos, 2, 0)]
    for d in (1, 2, 3):
        pairs = [(c, (c + d) % cols) for c in range(cols)]
        got.append(lax.ppermute(diagonal_for((pos + d) % cols), "col", pairs))
        wanted.append(lax.dynamic_slice_in_dim(upper, (pos + d) % cols, 2, 0))
    got, wanted = lax.optimization_barrier((got, wanted))
    for d in (1, 2, 3):
        pairs = [(c, (c + d) % cols) for c in range(cols) if (c + d) % 2 == 0]
        wanted[d] = lax.ppermute(wanted[d], "col", pairs)
    big = shape(NODES, NODES)
    ma, mb, u, logs, q = call(
        factor_first_kernel, (place, *got, rhs), FACTORS + (big,), WORK, scalars=1, flops=4 * 10**9
    )
    low, high = call(couple_first_kernel, (place, *wanted), (big, big), scalars=1, flops=10**6)
    kept, late = [], ()
    level = 0
    while (1 << level) < count:
        s = 1 << level
        leaving = [(2 * k + 1) * s - 1 for k in range(count // (2 * s))]
        even, uneven = leaving[0::2], leaving[1::2]
        odd = (((t + 1) // (2 * s)) % 2).astype(jnp.int32).reshape(1)
        last = 2 * s == count
        wn, ws, near = call(
            near_kernel,
            (odd, ma, mb, u, logs, q, low, high),
            (big, shape(NODES, TILE), big),
            scalars=1,
            flops=3 * 10**9,
        )
        arrived = [moved(near, [(i, i + s) for i in even])]
        if last:
            wf = jnp.zeros((NODES, NODES), F32)
            parts = (q, *arrived, *late)
        else:
            arrived.append(moved(near, [(i, i - s) for i in uneven]))
            n = len(late)
            wf, new, far, *q_adjusted = call(
                lambda *refs: far_kernel(n, *refs),
                (odd, ma, mb, u, logs, low, high, wn, ws, q, *late),
                (big,) * (4 if n else 3),
                scalars=1,
                flops=4 * 10**9,
            )
            q = q_adjusted[0] if n else q
            new, far, arrived = lax.optimization_barrier((new, far, arrived))
            parts = (q, *arrived)
            late = (
                moved(far, [(i, i - s) for i in even if i >= s]),
                moved(far, [(i, i + s) for i in uneven]),
            )
            low = moved(new, [(i, i + s) for i in even])
            high = moved(new, [(i, i - s) for i in uneven])
        mine = ((t + 1) % (2 * s) == s).astype(jnp.int32).reshape(1)
        flags = jnp.concatenate([mine, odd])
        kept.append((flags, s, (ma, mb, u, wn, wf, ws)))
        n_parts = len(parts)
        ma, mb, u, logs, q = call(
            lambda *refs: factor_next_kernel(n_parts, *refs),
            parts,
            FACTORS + (big,),
            WORK,
            flops=4 * 10**9,
        )
        level += 1
    whole_tip = jnp.eye(TILE, dtype=F32).at[0:effects, 0:effects].set(tip)
    whole_fixed = jnp.pad(rhs_fixed, (0, TILE - effects)).reshape(1, TILE)
    total = float(count * node_count + effects)
    (state,) = call(
        lambda *refs: root_kernel(total, *refs),
        (ma, mb, u, logs, q, whole_tip, whole_fixed),
        (shape(1, NODES + TILE),),
        ((NODES, TILE), (TILE, TILE)),
        flops=10**8,
    )
    for flags, s, factors in reversed(kept):
        leaving = [(2 * k + 1) * s - 1 for k in range(count // (2 * s))]
        from_left = moved(state, [(i - s, i) for i in leaving if i >= s])
        from_right = moved(state, [(i + s, i) for i in leaving])
        (state,) = call(
            back_kernel,
            (flags, from_left, from_right, state) + factors,
            (shape(1, NODES + TILE),),
            scalars=1,
            flops=10**7,
        )
    rows = lax.all_to_all(state[:, 0:NODES], "col", split_axis=1, concat_axis=0, tiled=True)
    rows = jnp.where(shift > 0, jnp.roll(rows, 2, axis=0), rows)
    return (rows, state[0, NODES : NODES + effects], state[0, NODES + 64])


def solution(mesh):
    placed = (
        P("tm", None, "col"),
        P("tm", None, "col"),
        P("tm", None, "col"),
        P(),
        P("tm", None),
        P(),
    )
    return jax.shard_map(
        per_device,
        mesh=mesh,
        in_specs=placed,
        out_specs=(P("tm", "col"), P(), P()),
        check_vma=False,
    )
```

```python
import jax
import jax.numpy as jnp
from jax import lax
from jax.experimental import pallas as pl
from jax.experimental.pallas import tpu as pltpu
from jax.sharding import PartitionSpec as P

AXES = ("tm", "col")
F32 = jnp.float32
TILE = 128
HALF = 256
NODES = 512
EFFECTS = 64


def mm(a, b):
    return lax.dot_general(
        a, b, (((1,), (0,)), ((), ())), precision=lax.Precision.HIGHEST, preferred_element_type=F32
    )


def mtm(a, b):
    return lax.dot_general(
        a, b, (((0,), (0,)), ((), ())), precision=lax.Precision.HIGHEST, preferred_element_type=F32
    )


def lane_splat(x, j):
    return jnp.broadcast_to(x[:, j : j + 1], (8, TILE))


def row_splat(x, i):
    return jnp.broadcast_to(x[i : i + 1, :], (8, TILE))


def factor_tile(tile, inv_ref, size):
    groups = size // 8
    a = [tile[8 * g : 8 * g + 8, :] for g in range(groups)]
    row = lax.broadcasted_iota(jnp.int32, (8, TILE), 0)
    lane = lax.broadcasted_iota(jnp.int32, (8, TILE), 1)
    inv = [jnp.where(lane == row + 8 * g, 1.0, 0.0).astype(F32) for g in range(groups)]
    pivots = jnp.ones((8, TILE), F32)
    for g0 in range(groups):
        top, side = a[g0], inv[g0]
        cols = [lane_splat(top, 8 * g0 + i) for i in range(8)]
        rows = [row_splat(top, i) for i in range(8)]
        side_rows = [row_splat(side, i) for i in range(8)]
        p = [[row_splat(cols[c], i) for c in range(i + 1)] for i in range(8)]
        low = [[None] * 8 for _ in range(8)]
        scale = []
        for c in range(8):
            r = lax.rsqrt(p[c][c])
            scale.append(r)
            pivots = jnp.where((row == c) & (lane == g0), p[c][c], pivots)
            for i in range(c + 1, 8):
                low[i][c] = p[i][c] * r
            for i in range(c + 1, 8):
                for k in range(c + 1, i + 1):
                    p[i][k] = p[i][k] - low[i][c] * low[k][c]
        u, v = [], []
        for i in range(8):
            x, y = rows[i], side_rows[i]
            for c in range(i):
                x = x - low[i][c] * u[c]
                y = y - low[i][c] * v[c]
            u.append(x * scale[i])
            v.append(y * scale[i])
        for g in range(g0 + 1, groups):
            e = []
            for i in range(8):
                x = lane_splat(a[g], 8 * g0 + i)
                for c in range(i):
                    x = x - low[i][c] * e[c]
                e.append(x * scale[i])
            for i in range(8):
                a[g] = a[g] - e[i] * u[i]
                inv[g] = inv[g] - e[i] * v[i]
        done = side
        for i in range(8):
            done = jnp.where(row == i, v[i], done)
        inv[g0] = done
    for g in range(groups):
        inv_ref[8 * g : 8 * g + 8, :] = inv[g]
    return pivots


def factor_body(s, inv, ma, mb, u):
    def body(k, logs):
        o = pl.multiple_of(k * TILE, TILE)
        pivots = factor_tile(s[pl.ds(o, TILE), pl.ds(o, TILE)], inv, TILE)
        for half, m in ((0, ma), (1, mb)):
            b0, b1, b2 = half * HALF, half * HALF + TILE, half * HALF + HALF

            @pl.when(k == 2 * half)
            def _():
                first = inv[...]
                panel = mm(first, s[b0:b1, b1:b2])
                s[b1:b2, b1:b2] = s[b1:b2, b1:b2] - mtm(panel, panel)
                m[0:TILE, 0:TILE] = first
                m[0:TILE, TILE:HALF] = jnp.zeros((TILE, TILE), F32)
                m[TILE:HALF, 0:TILE] = mtm(panel, first)

            @pl.when(k == 2 * half + 1)
            def _():
                second = inv[...]
                m[TILE:HALF, TILE:HALF] = second
                m[TILE:HALF, 0:TILE] = -mm(second, m[TILE:HALF, 0:TILE])
                if half == 0:
                    panel = mm(ma[...], s[0:HALF, HALF:NODES])
                    u[...] = panel
                    s[HALF:NODES, HALF:NODES] = s[HALF:NODES, HALF:NODES] - mtm(panel, panel)

        return logs + jnp.log(pivots)

    return lax.fori_loop(0, 4, body, jnp.zeros((8, TILE), F32))


def factor_first_kernel(flags, got, rhs, ma, mb, u, logs, q_new, s, inv):
    right = rhs[pl.ds(flags[2], 1), :]
    for k in range(4):
        s[:, k * TILE : (k + 1) * TILE] = got[k, 0:NODES, :]
    q_new[...] = s[...]
    q_new[TILE:HALF, 0:TILE] = jnp.zeros((TILE, TILE), F32)
    row = lax.broadcasted_iota(jnp.int32, (TILE - EFFECTS, TILE), 0)
    for k in range(4):
        part = jnp.broadcast_to(right[:, k * TILE : (k + 1) * TILE], row.shape)
        rest = jnp.where(row == 0, part, 0.0)
        edge = jnp.concatenate([got[k, NODES : NODES + EFFECTS, :], rest], axis=0).T
        o0, o1 = HALF + (k % 2) * TILE, (k // 2) * TILE
        q_new[o0 : o0 + TILE, o1 : o1 + TILE] = edge

    @pl.when(flags[0] != 0)
    def _():
        logs[...] = factor_body(s, inv, ma, mb, u)


def couple_first_kernel(flags, got, low, high):
    for k in range(4):
        high[:, k * TILE : (k + 1) * TILE] = got[k, 1]
        low[k * TILE : (k + 1) * TILE, :] = jnp.where(flags[3] > 0, got[k, 0].T, 0.0)


def factor_next_kernel(count, flags, *refs):
    parts, (ma, mb, u, logs, q_new, s, inv) = refs[:count], refs[count:]
    value = parts[0][...]
    for part in parts[1:]:
        value = value - part[...]
    q_new[...] = value

    @pl.when(flags[0] != 0)
    def _():
        s[...] = q_new[...]
        logs[...] = factor_body(s, inv, ma, mb, u)


def solve_into(ma, mb, u, top, bottom, out):
    first = mm(ma[...], top)
    out[0:HALF, :] = first
    out[HALF:NODES, :] = mm(mb[...], bottom - mtm(u[...], first))


def packed_products(w, ws, out, corner):
    whole, edge = w[...], ws[...]
    out[0:HALF, :] = mtm(w[:, 0:HALF], whole)
    out[HALF:NODES, HALF:NODES] = mtm(w[:, HALF:NODES], w[:, HALF:NODES])
    crossed = mtm(whole, edge)
    out[HALF:NODES, 0:TILE] = crossed[0:HALF]
    out[HALF:NODES, TILE:HALF] = crossed[HALF:NODES]
    out[TILE:HALF, 0:TILE] = corner


def corner_sums(q, ws, logs):
    row = lax.broadcasted_iota(jnp.int32, (TILE, TILE), 0)
    lane = lax.broadcasted_iota(jnp.int32, (TILE, TILE), 1)
    log_sum = jnp.sum(logs[...])
    sums = mtm(ws[...], ws[...]) - q[TILE:HALF, 0:TILE]
    return sums + jnp.where((row == 65) & (lane == 65), log_sum, 0.0)


def near_kernel(flags, ma, mb, u, logs, q, low, high, wn, ws, out):
    @pl.when(flags[0] != 0)
    def _():
        odd = flags[1] != 0
        pick = lambda rows: jnp.where(odd, low[rows, :], high[rows, :])
        solve_into(ma, mb, u, q[HALF:NODES, 0:TILE], q[HALF:NODES, TILE:HALF], ws)
        solve_into(ma, mb, u, pick(slice(0, HALF)), pick(slice(HALF, NODES)), wn)
        packed_products(wn, ws, out, jnp.where(odd, 0.0, corner_sums(q, ws, logs)))


def far_kernel(count, flags, ma, mb, u, logs, low, high, wn, ws, *refs):
    parts, outs = refs[: 1 + count], refs[1 + count :]
    wf, new, out = outs[:3]
    q = parts[0]

    @pl.when(flags[0] != 0)
    def _():
        odd = flags[1] != 0
        pick = lambda rows: jnp.where(odd, high[rows, :], low[rows, :])
        solve_into(ma, mb, u, pick(slice(0, HALF)), pick(slice(HALF, NODES)), wf)
        new[...] = -mtm(wn[...], wf[...])
        packed_products(wf, ws, out, jnp.where(odd, corner_sums(q, ws, logs), 0.0))

    if count:
        value = q[...]
        for part in parts[1:]:
            value = value - part[...]
        outs[3][...] = value


def back_solve(ma, mb, u, z_top, z_bottom):
    x_bottom = jnp.sum(mb[...] * z_bottom, axis=0, keepdims=True)
    z_top = z_top - jnp.sum(u[...] * x_bottom, axis=1, keepdims=True)
    x_top = jnp.sum(ma[...] * z_top, axis=0, keepdims=True)
    return x_top, x_bottom


def root_kernel(total, flags, ma, mb, u, logs, q, tip, fixed, out, ws, inv):
    @pl.when(flags[0] != 0)
    def _():
        root_body(total, ma, mb, u, logs, q, tip, fixed, out, ws, inv)


def root_body(total, ma, mb, u, logs, q, tip, fixed, out, ws, inv):
    solve_into(ma, mb, u, q[HALF:NODES, 0:TILE], q[HALF:NODES, TILE:HALF], ws)
    sums = corner_sums(q, ws, logs)
    row = lax.broadcasted_iota(jnp.int32, (TILE, TILE), 0)
    lane = lax.broadcasted_iota(jnp.int32, (TILE, TILE), 1)
    inv[...] = tip[...] - jnp.where((row < 64) & (lane < 64), sums, 0.0)
    pivots = factor_tile(inv[0:64, :], inv, 64)
    m = inv[0:64, :]
    rest = fixed[...] - sums[64:65, :]
    z = jnp.sum(m * rest, axis=1, keepdims=True)
    x_fixed = jnp.sum(m * z, axis=0, keepdims=True)
    lane1 = lax.broadcasted_iota(jnp.int32, (1, TILE), 1)
    x_fixed = jnp.where(lane1 < 64, x_fixed, 0.0)
    log_total = jnp.sum(jnp.where((row == 65) & (lane == 65), sums, 0.0)) + jnp.sum(jnp.log(pivots))
    weights = jnp.where(lane1 == 64, 1.0, -x_fixed)
    z = jnp.sum(ws[...] * weights, axis=1, keepdims=True)
    x_top, x_bottom = back_solve(ma, mb, u, z[0:HALF], z[HALF:NODES])
    out[:, 0:HALF] = x_top
    out[:, HALF:NODES] = x_bottom
    out[:, NODES : NODES + TILE] = jnp.where(lane1 == 64, log_total / total, x_fixed)


def back_kernel(flags, from_left, from_right, own, ma, mb, u, wn, wf, ws, out):
    lane1 = lax.broadcasted_iota(jnp.int32, (1, TILE), 1)
    extra = from_right[:, NODES : NODES + TILE]
    weights = jnp.where(lane1 == 64, 1.0, jnp.where(lane1 < 64, -extra, 0.0))
    odd = flags[1] != 0
    x_left, x_right = from_left[:, 0:NODES], from_right[:, 0:NODES]
    x_near, x_far = jnp.where(odd, x_left, x_right), jnp.where(odd, x_right, x_left)
    z = jnp.sum(ws[...] * weights, axis=1, keepdims=True) - jnp.sum(
        wn[...] * x_near + wf[...] * x_far, axis=1, keepdims=True
    )
    x_top, x_bottom = back_solve(ma, mb, u, z[0:HALF], z[HALF:NODES])
    mine = flags[0] != 0
    out[:, 0:HALF] = jnp.where(mine, x_top, own[:, 0:HALF])
    out[:, HALF:NODES] = jnp.where(mine, x_bottom, own[:, HALF:NODES])
    out[:, NODES : NODES + TILE] = jnp.where(mine, extra, own[:, NODES : NODES + TILE])


def shape(*dims):
    return jax.ShapeDtypeStruct(dims, F32)


def call(kernel, ins, outs, scratch=(), scalars=0, flops=0):
    smem = pl.BlockSpec(memory_space=pltpu.SMEM)
    vmem = pl.BlockSpec(memory_space=pltpu.VMEM)
    moved = 4 * sum(a.size for a in ins) + 4 * sum(o.size for o in outs)
    return pl.pallas_call(
        kernel,
        out_shape=tuple(outs),
        in_specs=[smem] * scalars + [vmem] * (len(ins) - scalars),
        out_specs=tuple([vmem] * len(outs)),
        scratch_shapes=[pltpu.VMEM(dims, F32) for dims in scratch],
        cost_estimate=pl.CostEstimate(flops=flops, bytes_accessed=moved, transcendentals=0),
    )(*ins)


FACTORS = (shape(HALF, HALF), shape(HALF, HALF), shape(HALF, HALF), shape(8, TILE))
WORK = ((NODES, NODES), (TILE, TILE))


def device_of(t):
    return (t // 4) * 4 + (t % 4 + 2 * ((t // 4) % 2)) % 4


def moved(x, pairs):
    return lax.ppermute(x, AXES, [(device_of(i), device_of(j)) for i, j in pairs])


def per_device(blocks, upper, arrow, tip, rhs, rhs_fixed):
    node_count = blocks.shape[1]
    effects = tip.shape[0]
    cols = 4
    count = lax.axis_size("tm") * cols
    col, shift = lax.axis_index("col"), 2 * (lax.axis_index("tm") % 2)
    pos = (col + shift) % cols
    t = lax.axis_index("tm") * cols + pos
    number = lambda *values: jnp.stack([jnp.asarray(v).astype(jnp.int32) for v in values])
    leaves = lambda s: (t + 1) % (2 * s) == s
    first = number(leaves(1), (t + 1) // 2 % 2, pos, t > 0)
    sent = jnp.concatenate([blocks, arrow], axis=1)
    sent = jnp.where(shift > 0, jnp.concatenate([sent[2:4], sent[0:2]], axis=0), sent)
    got = lax.all_to_all(sent, "col", split_axis=0, concat_axis=0, tiled=True)
    pairs = upper.reshape(2, 2, node_count, TILE)
    pairs = jnp.where(shift > 0, pairs[::-1], pairs)
    wanted = jnp.concatenate([pairs[:, None], jnp.zeros_like(pairs)[:, None]], axis=1)
    wanted = wanted.reshape(4, 2, node_count, TILE)
    got, wanted = lax.optimization_barrier((got, wanted))
    wanted = lax.all_to_all(wanted, "col", split_axis=0, concat_axis=0, tiled=True)
    big = shape(NODES, NODES)
    ma, mb, u, logs, q = call(
        factor_first_kernel, (first, got, rhs), FACTORS + (big,), WORK, scalars=1, flops=4 * 10**9
    )
    low, high = call(couple_first_kernel, (first, wanted), (big, big), scalars=1, flops=10**6)
    middle, upper_middle = count // 2 - 1, 3 * count // 4 - 1
    top_pairs = [(middle, upper_middle), (count - 1, middle), (upper_middle, count - 1)]
    kept, late = [], ()
    level = 0
    while (1 << level) < count:
        s = 1 << level
        leaving = [(2 * k + 1) * s - 1 for k in range(count // (2 * s))]
        even, uneven = leaving[0::2], leaving[1::2]
        flags = number(leaves(s), (t + 1) // (2 * s) % 2)
        last = 2 * s == count
        wn, ws, near = call(
            near_kernel,
            (flags, ma, mb, u, logs, q, low, high),
            (big, shape(NODES, TILE), big),
            scalars=1,
            flops=3 * 10**9,
        )
        arrived = [moved(near, [(i, i + s) for i in even])]
        if last:
            wf = jnp.zeros((NODES, NODES), F32)
            parts = (q, *arrived, *late)
        else:
            arrived.append(moved(near, [(i, i - s) for i in uneven]))
            n = len(late)
            wf, new, far, *q_adjusted = call(
                lambda *refs: far_kernel(n, *refs),
                (flags, ma, mb, u, logs, low, high, wn, ws, q, *late),
                (big,) * (4 if n else 3),
                scalars=1,
                flops=4 * 10**9,
            )
            q = q_adjusted[0] if n else q
            new, far, arrived = lax.optimization_barrier((new, far, arrived))
            parts = (q, *arrived)
            late = (moved(far, top_pairs if 4 * s == count else [(i, i + s) for i in uneven]),)
            if any(i >= s for i in even):
                late += (moved(far, [(i, i - s) for i in even if i >= s]),)
            low = moved(new, [(i, i + s) for i in even])
            high = moved(new, [(i, i - s) for i in uneven])
        kept.append((flags, s, (ma, mb, u, wn, wf, ws)))
        n_parts = len(parts)
        active = number(t == count - 1 if last else leaves(2 * s))
        ma, mb, u, logs, q = call(
            lambda *refs: factor_next_kernel(n_parts, *refs),
            (active, *parts),
            FACTORS + (big,),
            WORK,
            scalars=1,
            flops=4 * 10**9,
        )
        level += 1
    whole_tip = jnp.eye(TILE, dtype=F32).at[0:effects, 0:effects].set(tip)
    whole_fixed = jnp.pad(rhs_fixed, (0, TILE - effects)).reshape(1, TILE)
    total = float(count * node_count + effects)
    (state,) = call(
        lambda *refs: root_kernel(total, *refs),
        (active, ma, mb, u, logs, q, whole_tip, whole_fixed),
        (shape(1, NODES + TILE),),
        ((NODES, TILE), (TILE, TILE)),
        scalars=1,
        flops=10**8,
    )
    for flags, s, factors in reversed(kept):
        leaving = [(2 * k + 1) * s - 1 for k in range(count // (2 * s))]
        if 2 * s < count:
            pairs = [(i - s, i) for i in leaving if i >= s]
            from_left = moved(state, top_pairs if 4 * s == count else pairs)
            from_right = moved(state, [(i + s, i) for i in leaving])
        else:
            from_left = jnp.zeros_like(state)
            from_right = moved(state, top_pairs)
        (state,) = call(
            back_kernel,
            (flags, from_left, from_right, state) + factors,
            (shape(1, NODES + TILE),),
            scalars=1,
            flops=10**7,
        )
    rows = lax.all_to_all(state[:, 0:NODES], "col", split_axis=1, concat_axis=0, tiled=True)
    rows = jnp.where(shift > 0, jnp.roll(rows, 2, axis=0), rows)
    return (rows, state[0, NODES : NODES + effects], state[0, NODES + 64])


def solution(mesh):
    placed = (
        P("tm", None, "col"),
        P("tm", None, "col"),
        P("tm", None, "col"),
        P(),
        P("tm", None),
        P(),
    )
    return jax.shard_map(
        per_device,
        mesh=mesh,
        in_specs=placed,
        out_specs=(P("tm", "col"), P(), P()),
        check_vma=False,
    )
```

```python
import jax
import jax.numpy as jnp
from jax import lax
from jax.experimental import pallas as pl
from jax.experimental.pallas import tpu as pltpu
from jax.sharding import PartitionSpec as P

AXES = ("tm", "col")
F32 = jnp.float32
TILE = 128
HALF = 256
NODES = 512
EFFECTS = 64
UPPER = [(i, j) for i in range(4) for j in range(i, 4)]
SQUARE, EDGE, WHOLE = 10 * TILE, 5 * TILE, 16 * TILE


def mm(a, b):
    return lax.dot_general(
        a, b, (((1,), (0,)), ((), ())), precision=lax.Precision.HIGHEST, preferred_element_type=F32
    )


def mtm(a, b):
    return lax.dot_general(
        a, b, (((0,), (0,)), ((), ())), precision=lax.Precision.HIGHEST, preferred_element_type=F32
    )


def lane_splat(x, j):
    return jnp.broadcast_to(x[:, j : j + 1], (8, TILE))


def row_splat(x, i):
    return jnp.broadcast_to(x[i : i + 1, :], (8, TILE))


def factor_tile(tile, inv_ref, size):
    groups = size // 8
    a = [tile[8 * g : 8 * g + 8, :] for g in range(groups)]
    row = lax.broadcasted_iota(jnp.int32, (8, TILE), 0)
    lane = lax.broadcasted_iota(jnp.int32, (8, TILE), 1)
    inv = [jnp.where(lane == row + 8 * g, 1.0, 0.0).astype(F32) for g in range(groups)]
    pivots = jnp.ones((8, TILE), F32)
    for g0 in range(groups):
        top, side = a[g0], inv[g0]
        cols = [lane_splat(top, 8 * g0 + i) for i in range(8)]
        rows = [row_splat(top, i) for i in range(8)]
        side_rows = [row_splat(side, i) for i in range(8)]
        p = [[row_splat(cols[c], i) for c in range(i + 1)] for i in range(8)]
        low = [[None] * 8 for _ in range(8)]
        scale = []
        for c in range(8):
            r = lax.rsqrt(p[c][c])
            scale.append(r)
            pivots = jnp.where((row == c) & (lane == g0), p[c][c], pivots)
            for i in range(c + 1, 8):
                low[i][c] = p[i][c] * r
            for i in range(c + 1, 8):
                for k in range(c + 1, i + 1):
                    p[i][k] = p[i][k] - low[i][c] * low[k][c]
        u, v = [], []
        for i in range(8):
            x, y = rows[i], side_rows[i]
            for c in range(i):
                x = x - low[i][c] * u[c]
                y = y - low[i][c] * v[c]
            u.append(x * scale[i])
            v.append(y * scale[i])
        for g in range(g0 + 1, groups):
            e = []
            for i in range(8):
                x = lane_splat(a[g], 8 * g0 + i)
                for c in range(i):
                    x = x - low[i][c] * e[c]
                e.append(x * scale[i])
            for i in range(8):
                a[g] = a[g] - e[i] * u[i]
                inv[g] = inv[g] - e[i] * v[i]
        done = side
        for i in range(8):
            done = jnp.where(row == i, v[i], done)
        inv[g0] = done
    for g in range(groups):
        inv_ref[8 * g : 8 * g + 8, :] = inv[g]
    return pivots


def factor_body(s, inv, ma, mb, u):
    def body(k, logs):
        o = pl.multiple_of(k * TILE, TILE)
        pivots = factor_tile(s[pl.ds(o, TILE), pl.ds(o, TILE)], inv, TILE)
        for half, m in ((0, ma), (1, mb)):
            b0, b1, b2 = half * HALF, half * HALF + TILE, half * HALF + HALF

            @pl.when(k == 2 * half)
            def _():
                first = inv[...]
                panel = mm(first, s[b0:b1, b1:b2])
                s[b1:b2, b1:b2] = s[b1:b2, b1:b2] - mtm(panel, panel)
                m[0:TILE, 0:TILE] = first
                m[0:TILE, TILE:HALF] = jnp.zeros((TILE, TILE), F32)
                m[TILE:HALF, 0:TILE] = mtm(panel, first)

            @pl.when(k == 2 * half + 1)
            def _():
                second = inv[...]
                m[TILE:HALF, TILE:HALF] = second
                m[TILE:HALF, 0:TILE] = -mm(second, m[TILE:HALF, 0:TILE])
                if half == 0:
                    panel = mm(ma[...], s[0:HALF, HALF:NODES])
                    u[...] = panel
                    s[HALF:NODES, HALF:NODES] = s[HALF:NODES, HALF:NODES] - mtm(panel, panel)

        return logs + jnp.log(pivots)

    return lax.fori_loop(0, 4, body, jnp.zeros((8, TILE), F32))


def block_rows(index, base=0):
    return slice(base + index * TILE, base + (index + 1) * TILE)


def factor_first_kernel(flags, got, rhs, ma, mb, u, logs, q, s, inv):
    right = rhs[pl.ds(flags[2], 1), :]
    for k in range(4):
        s[:, k * TILE : (k + 1) * TILE] = got[k, 0:NODES, :]
    for b, (i, j) in enumerate(UPPER):
        q[block_rows(b), :] = got[j, block_rows(i), :]
    row = lax.broadcasted_iota(jnp.int32, (TILE - EFFECTS, TILE), 0)
    for k in range(4):
        part = jnp.broadcast_to(right[:, k * TILE : (k + 1) * TILE], row.shape)
        rest = jnp.where(row == 0, part, 0.0)
        edge = jnp.concatenate([got[k, NODES : NODES + EFFECTS, :], rest], axis=0).T
        q[block_rows(k, SQUARE), :] = edge
    q[block_rows(4, SQUARE), :] = jnp.zeros((TILE, TILE), F32)

    @pl.when(flags[0] != 0)
    def _():
        logs[...] = factor_body(s, inv, ma, mb, u)


def couple_first_kernel(flags, got, low, high):
    for k in range(4):
        high[k * NODES : (k + 1) * NODES, :] = got[k, 1]
        turned = jnp.where(flags[3] > 0, got[k, 0].T, 0.0)
        for j in range(4):
            o = j * NODES + k * TILE
            low[o : o + TILE, :] = turned[:, j * TILE : (j + 1) * TILE]
    for ref in (low, high):
        ref[WHOLE : WHOLE + EDGE, :] = jnp.zeros((EDGE, TILE), F32)


def factor_next_kernel(count, flags, *refs):
    parts, (ma, mb, u, logs, s, inv) = refs[:count], refs[count:]

    @pl.when(flags[0] != 0)
    def _():
        for b, (i, j) in enumerate(UPPER):
            value = parts[0][block_rows(b), :]
            for part in parts[1:]:
                value = value - part[block_rows(b), :]
            s[block_rows(i), j * TILE : (j + 1) * TILE] = value
        logs[...] = factor_body(s, inv, ma, mb, u)


def solve_into(ma, mb, u, top, bottom, out):
    first = mm(ma[...], top)
    out[0:HALF, :] = first
    out[HALF:NODES, :] = mm(mb[...], bottom - mtm(u[...], first))


def square_products(w, out):
    top = mtm(w[:, 0:HALF], w[...])
    bottom = mtm(w[:, HALF:NODES], w[:, HALF:NODES])
    for b, (i, j) in enumerate(UPPER):
        rows, cols = block_rows(i % 2), slice(j * TILE, (j + 1) * TILE)
        if i < 2:
            out[block_rows(b), :] = top[rows, cols]
        else:
            out[block_rows(b), :] = bottom[rows, block_rows(j - 2)]


def corner_sums(corner, ws, logs):
    row = lax.broadcasted_iota(jnp.int32, (TILE, TILE), 0)
    lane = lax.broadcasted_iota(jnp.int32, (TILE, TILE), 1)
    log_sum = jnp.sum(logs[...])
    sums = mtm(ws[...], ws[...]) - corner
    return sums + jnp.where((row == 65) & (lane == 65), log_sum, 0.0)


def solve_columns(ma, mb, u, flag, first, second, out):
    def rows(o):
        at = [slice(k * NODES + o, k * NODES + o + HALF) for k in range(4)]
        return jnp.concatenate([jnp.where(flag, first[r, :], second[r, :]) for r in at], axis=1)

    solve_into(ma, mb, u, rows(0), rows(HALF), out)


def near_kernel(flags, ma, mb, u, low, high, wn, out):
    @pl.when(flags[0] != 0)
    def _():
        solve_columns(ma, mb, u, flags[1] != 0, low, high, wn)
        square_products(wn, out)


def edge_part(parts, o, n):
    value = parts[0][SQUARE + o : SQUARE + o + n, :]
    for part, base in parts[1:]:
        value = value - part[base + o : base + o + n, :]
    return value


def far_kernel(count, flags, ma, mb, u, logs, low, high, wn, *refs):
    parts, outs = refs[: 1 + count], refs[1 + count :]
    wf, ws, new, out = outs[:4]
    q = parts[0]

    @pl.when(flags[0] != 0)
    def _():
        odd = flags[1] != 0
        edge = lambda o, n: edge_part((q, (low, WHOLE), (high, WHOLE)), o, n)
        solve_columns(ma, mb, u, odd, high, low, wf)
        product = -mtm(wn[...], wf[...])
        for k in range(4):
            new[k * NODES : (k + 1) * NODES, :] = product[:, k * TILE : (k + 1) * TILE]
        solve_into(ma, mb, u, edge(0, HALF), edge(HALF, HALF), ws)
        corner = corner_sums(edge(NODES, TILE), ws, logs)
        new[WHOLE : WHOLE + NODES, :] = mtm(wn[...], ws[...])
        new[WHOLE + NODES : WHOLE + EDGE, :] = jnp.where(odd, 0.0, corner)
        square_products(wf, out)
        out[SQUARE : SQUARE + NODES, :] = mtm(wf[...], ws[...])
        out[SQUARE + NODES : SQUARE + EDGE, :] = jnp.where(odd, corner, 0.0)

    if count:
        value = q[...]
        for part in parts[1:]:
            value = value - part[...]
        outs[4][...] = value


def last_kernel(flags, ma, mb, u, logs, low, high, wn, q, ws, out):
    @pl.when(flags[0] != 0)
    def _():
        edge = lambda o, n: edge_part((q, (low, WHOLE), (high, WHOLE)), o, n)
        solve_into(ma, mb, u, edge(0, HALF), edge(HALF, HALF), ws)
        out[0:NODES, :] = mtm(wn[...], ws[...])
        out[NODES:EDGE, :] = corner_sums(edge(NODES, TILE), ws, logs)


def back_solve(ma, mb, u, z_top, z_bottom):
    x_bottom = jnp.sum(mb[...] * z_bottom, axis=0, keepdims=True)
    z_top = z_top - jnp.sum(u[...] * x_bottom, axis=1, keepdims=True)
    x_top = jnp.sum(ma[...] * z_top, axis=0, keepdims=True)
    return x_top, x_bottom


def root_kernel(total, count, flags, ma, mb, u, logs, tip, fixed, last, q, *refs):
    @pl.when(flags[0] != 0)
    def _():
        parts = (q, (last, 0), *((part, SQUARE) for part in refs[:count]))
        root_body(total, ma, mb, u, logs, parts, tip, fixed, *refs[count:])


def root_body(total, ma, mb, u, logs, parts, tip, fixed, out, ws, inv):
    solve_into(ma, mb, u, edge_part(parts, 0, HALF), edge_part(parts, HALF, HALF), ws)
    sums = corner_sums(edge_part(parts, NODES, TILE), ws, logs)
    row = lax.broadcasted_iota(jnp.int32, (TILE, TILE), 0)
    lane = lax.broadcasted_iota(jnp.int32, (TILE, TILE), 1)
    inv[...] = tip[...] - jnp.where((row < 64) & (lane < 64), sums, 0.0)
    pivots = factor_tile(inv[0:64, :], inv, 64)
    m = inv[0:64, :]
    rest = fixed[...] - sums[64:65, :]
    z = jnp.sum(m * rest, axis=1, keepdims=True)
    x_fixed = jnp.sum(m * z, axis=0, keepdims=True)
    lane1 = lax.broadcasted_iota(jnp.int32, (1, TILE), 1)
    x_fixed = jnp.where(lane1 < 64, x_fixed, 0.0)
    log_total = jnp.sum(jnp.where((row == 65) & (lane == 65), sums, 0.0)) + jnp.sum(jnp.log(pivots))
    weights = jnp.where(lane1 == 64, 1.0, -x_fixed)
    z = jnp.sum(ws[...] * weights, axis=1, keepdims=True)
    x_top, x_bottom = back_solve(ma, mb, u, z[0:HALF], z[HALF:NODES])
    out[:, 0:HALF] = x_top
    out[:, HALF:NODES] = x_bottom
    out[:, NODES : NODES + TILE] = jnp.where(lane1 == 64, log_total / total, x_fixed)


def back_kernel(flags, from_left, from_right, own, ma, mb, u, wn, wf, ws, out):
    lane1 = lax.broadcasted_iota(jnp.int32, (1, TILE), 1)
    extra = from_right[:, NODES : NODES + TILE]
    weights = jnp.where(lane1 == 64, 1.0, jnp.where(lane1 < 64, -extra, 0.0))
    odd = flags[1] != 0
    x_left, x_right = from_left[:, 0:NODES], from_right[:, 0:NODES]
    x_near, x_far = jnp.where(odd, x_left, x_right), jnp.where(odd, x_right, x_left)
    z = jnp.sum(ws[...] * weights, axis=1, keepdims=True) - jnp.sum(
        wn[...] * x_near + wf[...] * x_far, axis=1, keepdims=True
    )
    x_top, x_bottom = back_solve(ma, mb, u, z[0:HALF], z[HALF:NODES])
    mine = flags[0] != 0
    out[:, 0:HALF] = jnp.where(mine, x_top, own[:, 0:HALF])
    out[:, HALF:NODES] = jnp.where(mine, x_bottom, own[:, HALF:NODES])
    out[:, NODES : NODES + TILE] = jnp.where(mine, extra, own[:, NODES : NODES + TILE])


def shape(*dims):
    return jax.ShapeDtypeStruct(dims, F32)


def call(kernel, ins, outs, scratch=(), scalars=0, flops=0):
    smem = pl.BlockSpec(memory_space=pltpu.SMEM)
    vmem = pl.BlockSpec(memory_space=pltpu.VMEM)
    moved = 4 * sum(a.size for a in ins) + 4 * sum(o.size for o in outs)
    return pl.pallas_call(
        kernel,
        out_shape=tuple(outs),
        in_specs=[smem] * scalars + [vmem] * (len(ins) - scalars),
        out_specs=tuple([vmem] * len(outs)),
        scratch_shapes=[pltpu.VMEM(dims, F32) for dims in scratch],
        cost_estimate=pl.CostEstimate(flops=flops, bytes_accessed=moved, transcendentals=0),
    )(*ins)


FACTORS = (shape(HALF, HALF), shape(HALF, HALF), shape(HALF, HALF), shape(8, TILE))
WORK = ((NODES, NODES), (TILE, TILE))


def device_of(t):
    return (t // 4) * 4 + (t % 4 + 2 * ((t // 4) % 2)) % 4


def moved(x, pairs):
    return lax.ppermute(x, AXES, [(device_of(i), device_of(j)) for i, j in pairs])


def per_device(blocks, upper, arrow, tip, rhs, rhs_fixed):
    node_count = blocks.shape[1]
    effects = tip.shape[0]
    cols = 4
    count = lax.axis_size("tm") * cols
    col, shift = lax.axis_index("col"), 2 * (lax.axis_index("tm") % 2)
    pos = (col + shift) % cols
    t = lax.axis_index("tm") * cols + pos
    number = lambda *values: jnp.stack([jnp.asarray(v).astype(jnp.int32) for v in values])
    leaves = lambda s: (t + 1) % (2 * s) == s
    first = number(leaves(1), (t + 1) // 2 % 2, pos, t > 0)
    sent = jnp.concatenate([blocks, arrow], axis=1)
    sent = jnp.where(shift > 0, jnp.concatenate([sent[2:4], sent[0:2]], axis=0), sent)
    got = lax.all_to_all(sent, "col", split_axis=0, concat_axis=0, tiled=True)
    pairs = upper.reshape(2, 2, node_count, TILE)
    pairs = jnp.where(shift > 0, pairs[::-1], pairs)
    wanted = jnp.concatenate([pairs[:, None], jnp.zeros_like(pairs)[:, None]], axis=1)
    wanted = wanted.reshape(4, 2, node_count, TILE)
    got, wanted = lax.optimization_barrier((got, wanted))
    wanted = lax.all_to_all(wanted, "col", split_axis=0, concat_axis=0, tiled=True)
    big, thin = shape(NODES, NODES), shape(NODES, TILE)
    state_shape, coupled = shape(SQUARE + EDGE, TILE), shape(WHOLE + EDGE, TILE)
    ma, mb, u, logs, q = call(
        factor_first_kernel,
        (first, got, rhs),
        FACTORS + (state_shape,),
        WORK,
        scalars=1,
        flops=4 * 10**9,
    )
    low, high = call(
        couple_first_kernel, (first, wanted), (coupled, coupled), scalars=1, flops=10**6
    )
    middle, upper_middle = count // 2 - 1, 3 * count // 4 - 1
    top_pairs = [(middle, upper_middle), (count - 1, middle), (upper_middle, count - 1)]
    kept, late = [], ()
    level = 0
    while (1 << level) < count:
        s = 1 << level
        leaving = [(2 * k + 1) * s - 1 for k in range(count // (2 * s))]
        even, uneven = leaving[0::2], leaving[1::2]
        flags = number(leaves(s), (t + 1) // (2 * s) % 2)
        last = 2 * s == count
        wn, near = call(
            near_kernel,
            (flags, ma, mb, u, low, high),
            (big, shape(SQUARE, TILE)),
            scalars=1,
            flops=3 * 10**9,
        )
        arrived = [moved(near, [(i, i + s) for i in even])]
        if last:
            wf = jnp.zeros((NODES, NODES), F32)
            ws, edge = call(
                last_kernel,
                (flags, ma, mb, u, logs, low, high, wn, q),
                (thin, shape(EDGE, TILE)),
                scalars=1,
                flops=10**9,
            )
            edge, arrived = lax.optimization_barrier((edge, arrived))
            edge = moved(edge, [(i, i + s) for i in even])
            parts = (q, *arrived, *late)
        else:
            arrived.append(moved(near, [(i, i - s) for i in uneven]))
            n = len(late)
            wf, ws, new, far, *q_adjusted = call(
                lambda *refs: far_kernel(n, *refs),
                (flags, ma, mb, u, logs, low, high, wn, q, *late),
                (big, thin, coupled, state_shape) + (state_shape,) * (1 if n else 0),
                scalars=1,
                flops=4 * 10**9,
            )
            q = q_adjusted[0] if n else q
            new, arrived = lax.optimization_barrier((new, arrived))
            parts = (q, *arrived)
            late = (moved(far, top_pairs if 4 * s == count else [(i, i + s) for i in uneven]),)
            if any(i >= s for i in even):
                late += (moved(far, [(i, i - s) for i in even if i >= s]),)
            low = moved(new, [(i, i + s) for i in even])
            high = moved(new, [(i, i - s) for i in uneven])
        kept.append((flags, s, (ma, mb, u, wn, wf, ws)))
        n_parts = len(parts)
        active = number(t == count - 1 if last else leaves(2 * s))
        ma, mb, u, logs = call(
            lambda *refs: factor_next_kernel(n_parts, *refs),
            (active, *parts),
            FACTORS,
            WORK,
            scalars=1,
            flops=4 * 10**9,
        )
        level += 1
    whole_tip = jnp.eye(TILE, dtype=F32).at[0:effects, 0:effects].set(tip)
    whole_fixed = jnp.pad(rhs_fixed, (0, TILE - effects)).reshape(1, TILE)
    total = float(count * node_count + effects)
    n_late = len(late)
    (state,) = call(
        lambda *refs: root_kernel(total, n_late, *refs),
        (active, ma, mb, u, logs, whole_tip, whole_fixed, edge, q, *late),
        (shape(1, NODES + TILE),),
        ((NODES, TILE), (TILE, TILE)),
        scalars=1,
        flops=10**8,
    )
    for flags, s, factors in reversed(kept):
        leaving = [(2 * k + 1) * s - 1 for k in range(count // (2 * s))]
        if 2 * s < count:
            pairs = [(i - s, i) for i in leaving if i >= s]
            from_left = moved(state, top_pairs if 4 * s == count else pairs)
            from_right = moved(state, [(i + s, i) for i in leaving])
        else:
            from_left = jnp.zeros_like(state)
            from_right = moved(state, top_pairs)
        (state,) = call(
            back_kernel,
            (flags, from_left, from_right, state) + factors,
            (shape(1, NODES + TILE),),
            scalars=1,
            flops=10**7,
        )
    rows = lax.all_to_all(state[:, 0:NODES], "col", split_axis=1, concat_axis=0, tiled=True)
    rows = jnp.where(shift > 0, jnp.roll(rows, 2, axis=0), rows)
    return (rows, state[0, NODES : NODES + effects], state[0, NODES + 64])


def solution(mesh):
    placed = (
        P("tm", None, "col"),
        P("tm", None, "col"),
        P("tm", None, "col"),
        P(),
        P("tm", None),
        P(),
    )
    return jax.shard_map(
        per_device,
        mesh=mesh,
        in_specs=placed,
        out_specs=(P("tm", "col"), P(), P()),
        check_vma=False,
    )
```

```python
import jax
import jax.numpy as jnp
from jax import lax
from jax.experimental import pallas as pl
from jax.experimental.pallas import tpu as pltpu
from jax.sharding import PartitionSpec as P

AXES = ("tm", "col")
F32 = jnp.float32
TILE = 128
HALF = 256
NODES = 512
EFFECTS = 64
UPPER = [(i, j) for i in range(4) for j in range(i, 4)]
SQUARE, EDGE, WHOLE = 10 * TILE, 5 * TILE, 16 * TILE


def mm(a, b):
    return lax.dot_general(
        a, b, (((1,), (0,)), ((), ())), precision=lax.Precision.HIGHEST, preferred_element_type=F32
    )


def mtm(a, b):
    return lax.dot_general(
        a, b, (((0,), (0,)), ((), ())), precision=lax.Precision.HIGHEST, preferred_element_type=F32
    )


def lane_splat(x, j):
    return jnp.broadcast_to(x[:, j : j + 1], (8, TILE))


def row_splat(x, i):
    return jnp.broadcast_to(x[i : i + 1, :], (8, TILE))


def factor_tile(tile, inv_ref, size):
    groups = size // 8
    a = [tile[8 * g : 8 * g + 8, :] for g in range(groups)]
    row = lax.broadcasted_iota(jnp.int32, (8, TILE), 0)
    lane = lax.broadcasted_iota(jnp.int32, (8, TILE), 1)
    inv = [jnp.where(lane == row + 8 * g, 1.0, 0.0).astype(F32) for g in range(groups)]
    pivots = jnp.ones((8, TILE), F32)
    for g0 in range(groups):
        top, side = a[g0], inv[g0]
        cols = [lane_splat(top, 8 * g0 + i) for i in range(8)]
        rows = [row_splat(top, i) for i in range(8)]
        side_rows = [row_splat(side, i) for i in range(8)]
        p = [[row_splat(cols[c], i) for c in range(i + 1)] for i in range(8)]
        low = [[None] * 8 for _ in range(8)]
        scale = []
        for c in range(8):
            r = lax.rsqrt(p[c][c])
            scale.append(r)
            pivots = jnp.where((row == c) & (lane == g0), p[c][c], pivots)
            for i in range(c + 1, 8):
                low[i][c] = p[i][c] * r
            for i in range(c + 1, 8):
                for k in range(c + 1, i + 1):
                    p[i][k] = p[i][k] - low[i][c] * low[k][c]
        u, v = [], []
        for i in range(8):
            x, y = rows[i], side_rows[i]
            for c in range(i):
                x = x - low[i][c] * u[c]
                y = y - low[i][c] * v[c]
            u.append(x * scale[i])
            v.append(y * scale[i])
        for g in range(g0 + 1, groups):
            e = []
            for i in range(8):
                x = lane_splat(a[g], 8 * g0 + i)
                for c in range(i):
                    x = x - low[i][c] * e[c]
                e.append(x * scale[i])
            for i in range(8):
                a[g] = a[g] - e[i] * u[i]
                inv[g] = inv[g] - e[i] * v[i]
        done = side
        for i in range(8):
            done = jnp.where(row == i, v[i], done)
        inv[g0] = done
    for g in range(groups):
        inv_ref[8 * g : 8 * g + 8, :] = inv[g]
    return pivots


def factor_body(s, inv, ma, mb, u):
    def body(k, logs):
        o = pl.multiple_of(k * TILE, TILE)
        pivots = factor_tile(s[pl.ds(o, TILE), pl.ds(o, TILE)], inv, TILE)
        for half, m in ((0, ma), (1, mb)):
            b0, b1, b2 = half * HALF, half * HALF + TILE, half * HALF + HALF

            @pl.when(k == 2 * half)
            def _():
                first = inv[...]
                panel = mm(first, s[b0:b1, b1:b2])
                s[b1:b2, b1:b2] = s[b1:b2, b1:b2] - mtm(panel, panel)
                m[0:TILE, 0:TILE] = first
                m[0:TILE, TILE:HALF] = jnp.zeros((TILE, TILE), F32)
                m[TILE:HALF, 0:TILE] = mtm(panel, first)

            @pl.when(k == 2 * half + 1)
            def _():
                second = inv[...]
                m[TILE:HALF, TILE:HALF] = second
                m[TILE:HALF, 0:TILE] = -mm(second, m[TILE:HALF, 0:TILE])
                if half == 0:
                    panel = mm(ma[...], s[0:HALF, HALF:NODES])
                    u[...] = panel
                    s[HALF:NODES, HALF:NODES] = s[HALF:NODES, HALF:NODES] - mtm(panel, panel)

        return logs + jnp.log(pivots)

    return lax.fori_loop(0, 4, body, jnp.zeros((8, TILE), F32))


def block_rows(index, base=0):
    return slice(base + index * TILE, base + (index + 1) * TILE)


def factor_first_kernel(place, flags, got, rhs, ma, mb, u, logs, q, s, inv):
    right = rhs[pl.ds(flags[place], 1), :]
    for k in range(4):
        s[:, k * TILE : (k + 1) * TILE] = got[k, 0:NODES, :]
    for b, (i, j) in enumerate(UPPER):
        q[block_rows(b), :] = got[j, block_rows(i), :]
    row = lax.broadcasted_iota(jnp.int32, (TILE - EFFECTS, TILE), 0)
    for k in range(4):
        part = jnp.broadcast_to(right[:, k * TILE : (k + 1) * TILE], row.shape)
        rest = jnp.where(row == 0, part, 0.0)
        edge = jnp.concatenate([got[k, NODES : NODES + EFFECTS, :], rest], axis=0).T
        q[block_rows(k, SQUARE), :] = edge
    q[block_rows(4, SQUARE), :] = jnp.zeros((TILE, TILE), F32)

    @pl.when(flags[0] != 0)
    def _():
        logs[...] = factor_body(s, inv, ma, mb, u)


def couple_first_kernel(place, flags, got, low, high):
    for k in range(4):
        high[k * NODES : (k + 1) * NODES, :] = got[k, 1]
        turned = jnp.where(flags[place + 1] > 0, got[k, 0].T, 0.0)
        for j in range(4):
            o = j * NODES + k * TILE
            low[o : o + TILE, :] = turned[:, j * TILE : (j + 1) * TILE]
    for ref in (low, high):
        ref[WHOLE : WHOLE + EDGE, :] = jnp.zeros((EDGE, TILE), F32)


def factor_next_kernel(count, flags, *refs):
    parts, (ma, mb, u, logs, s, inv) = refs[:count], refs[count:]

    @pl.when(flags[0] != 0)
    def _():
        for b, (i, j) in enumerate(UPPER):
            value = parts[0][block_rows(b), :]
            for part in parts[1:]:
                value = value - part[block_rows(b), :]
            s[block_rows(i), j * TILE : (j + 1) * TILE] = value
        logs[...] = factor_body(s, inv, ma, mb, u)


def solve_into(ma, mb, u, top, bottom, out):
    first = mm(ma[...], top)
    out[0:HALF, :] = first
    out[HALF:NODES, :] = mm(mb[...], bottom - mtm(u[...], first))


def square_products(w, out):
    top = mtm(w[:, 0:HALF], w[...])
    bottom = mtm(w[:, HALF:NODES], w[:, HALF:NODES])
    for b, (i, j) in enumerate(UPPER):
        rows, cols = block_rows(i % 2), slice(j * TILE, (j + 1) * TILE)
        if i < 2:
            out[block_rows(b), :] = top[rows, cols]
        else:
            out[block_rows(b), :] = bottom[rows, block_rows(j - 2)]


def corner_sums(corner, ws, logs):
    row = lax.broadcasted_iota(jnp.int32, (TILE, TILE), 0)
    lane = lax.broadcasted_iota(jnp.int32, (TILE, TILE), 1)
    log_sum = jnp.sum(logs[...])
    sums = mtm(ws[...], ws[...]) - corner
    return sums + jnp.where((row == 65) & (lane == 65), log_sum, 0.0)


def solve_columns(ma, mb, u, flag, first, second, out):
    def rows(o):
        at = [slice(k * NODES + o, k * NODES + o + HALF) for k in range(4)]
        return jnp.concatenate([jnp.where(flag, first[r, :], second[r, :]) for r in at], axis=1)

    solve_into(ma, mb, u, rows(0), rows(HALF), out)


def near_kernel(flags, ma, mb, u, low, high, wn, out):
    @pl.when(flags[0] != 0)
    def _():
        solve_columns(ma, mb, u, flags[1] != 0, low, high, wn)
        square_products(wn, out)


def edge_part(parts, o, n):
    value = parts[0][SQUARE + o : SQUARE + o + n, :]
    for part, base in parts[1:]:
        value = value - part[base + o : base + o + n, :]
    return value


def far_kernel(count, flags, ma, mb, u, logs, low, high, wn, *refs):
    parts, outs = refs[: 1 + count], refs[1 + count :]
    wf, ws, new, out = outs[:4]
    q = parts[0]

    @pl.when(flags[0] != 0)
    def _():
        odd = flags[1] != 0
        edge = lambda o, n: edge_part((q, (low, WHOLE), (high, WHOLE)), o, n)
        solve_columns(ma, mb, u, odd, high, low, wf)
        product = -mtm(wn[...], wf[...])
        for k in range(4):
            new[k * NODES : (k + 1) * NODES, :] = product[:, k * TILE : (k + 1) * TILE]
        solve_into(ma, mb, u, edge(0, HALF), edge(HALF, HALF), ws)
        corner = corner_sums(edge(NODES, TILE), ws, logs)
        new[WHOLE : WHOLE + NODES, :] = mtm(wn[...], ws[...])
        new[WHOLE + NODES : WHOLE + EDGE, :] = jnp.where(odd, 0.0, corner)
        square_products(wf, out)
        out[SQUARE : SQUARE + NODES, :] = mtm(wf[...], ws[...])
        out[SQUARE + NODES : SQUARE + EDGE, :] = jnp.where(odd, corner, 0.0)

    if count:
        value = q[...]
        for part in parts[1:]:
            value = value - part[...]
        outs[4][...] = value


def last_kernel(flags, ma, mb, u, logs, low, high, wn, q, ws, out):
    @pl.when(flags[0] != 0)
    def _():
        edge = lambda o, n: edge_part((q, (low, WHOLE), (high, WHOLE)), o, n)
        solve_into(ma, mb, u, edge(0, HALF), edge(HALF, HALF), ws)
        out[0:NODES, :] = mtm(wn[...], ws[...])
        out[NODES:EDGE, :] = corner_sums(edge(NODES, TILE), ws, logs)


def back_solve(ma, mb, u, z_top, z_bottom):
    x_bottom = jnp.sum(mb[...] * z_bottom, axis=0, keepdims=True)
    z_top = z_top - jnp.sum(u[...] * x_bottom, axis=1, keepdims=True)
    x_top = jnp.sum(ma[...] * z_top, axis=0, keepdims=True)
    return x_top, x_bottom


def root_kernel(total, count, flags, ma, mb, u, logs, tip, fixed, last, q, *refs):
    @pl.when(flags[0] != 0)
    def _():
        parts = (q, (last, 0), *((part, SQUARE) for part in refs[:count]))
        root_body(total, ma, mb, u, logs, parts, tip, fixed, *refs[count:])


def root_body(total, ma, mb, u, logs, parts, tip, fixed, out, ws, inv):
    solve_into(ma, mb, u, edge_part(parts, 0, HALF), edge_part(parts, HALF, HALF), ws)
    sums = corner_sums(edge_part(parts, NODES, TILE), ws, logs)
    row = lax.broadcasted_iota(jnp.int32, (TILE, TILE), 0)
    lane = lax.broadcasted_iota(jnp.int32, (TILE, TILE), 1)
    inv[...] = tip[...] - jnp.where((row < 64) & (lane < 64), sums, 0.0)
    pivots = factor_tile(inv[0:64, :], inv, 64)
    m = inv[0:64, :]
    rest = fixed[...] - sums[64:65, :]
    z = jnp.sum(m * rest, axis=1, keepdims=True)
    x_fixed = jnp.sum(m * z, axis=0, keepdims=True)
    lane1 = lax.broadcasted_iota(jnp.int32, (1, TILE), 1)
    x_fixed = jnp.where(lane1 < 64, x_fixed, 0.0)
    log_total = jnp.sum(jnp.where((row == 65) & (lane == 65), sums, 0.0)) + jnp.sum(jnp.log(pivots))
    weights = jnp.where(lane1 == 64, 1.0, -x_fixed)
    z = jnp.sum(ws[...] * weights, axis=1, keepdims=True)
    x_top, x_bottom = back_solve(ma, mb, u, z[0:HALF], z[HALF:NODES])
    out[:, 0:HALF] = x_top
    out[:, HALF:NODES] = x_bottom
    out[:, NODES : NODES + TILE] = jnp.where(lane1 == 64, log_total / total, x_fixed)


def back_kernel(flags, from_left, from_right, own, ma, mb, u, wn, wf, ws, out):
    lane1 = lax.broadcasted_iota(jnp.int32, (1, TILE), 1)
    extra = from_right[:, NODES : NODES + TILE]
    weights = jnp.where(lane1 == 64, 1.0, jnp.where(lane1 < 64, -extra, 0.0))
    odd = flags[1] != 0
    x_left, x_right = from_left[:, 0:NODES], from_right[:, 0:NODES]
    x_near, x_far = jnp.where(odd, x_left, x_right), jnp.where(odd, x_right, x_left)
    z = jnp.sum(ws[...] * weights, axis=1, keepdims=True) - jnp.sum(
        wn[...] * x_near + wf[...] * x_far, axis=1, keepdims=True
    )
    x_top, x_bottom = back_solve(ma, mb, u, z[0:HALF], z[HALF:NODES])
    mine = flags[0] != 0
    out[:, 0:HALF] = jnp.where(mine, x_top, own[:, 0:HALF])
    out[:, HALF:NODES] = jnp.where(mine, x_bottom, own[:, HALF:NODES])
    out[:, NODES : NODES + TILE] = jnp.where(mine, extra, own[:, NODES : NODES + TILE])


def shape(*dims):
    return jax.ShapeDtypeStruct(dims, F32)


class Entries:
    def __init__(self, table, base):
        self.table, self.base = table, base

    def __getitem__(self, k):
        return self.table[self.base + k]


def call(kernel, base, ins, outs, scratch=(), flops=0):
    smem = pl.BlockSpec(memory_space=pltpu.SMEM)
    vmem = pl.BlockSpec(memory_space=pltpu.VMEM)
    moved = 4 * sum(a.size for a in ins) + 4 * sum(o.size for o in outs)
    return pl.pallas_call(
        lambda table, *refs: kernel(Entries(table, base), *refs),
        out_shape=tuple(outs),
        in_specs=[smem] + [vmem] * (len(ins) - 1),
        out_specs=tuple([vmem] * len(outs)),
        scratch_shapes=[pltpu.VMEM(dims, F32) for dims in scratch],
        cost_estimate=pl.CostEstimate(flops=flops, bytes_accessed=moved, transcendentals=0),
    )(*ins)


FACTORS = (shape(HALF, HALF), shape(HALF, HALF), shape(HALF, HALF), shape(8, TILE))
WORK = ((NODES, NODES), (TILE, TILE))


def device_of(t):
    return (t // 4) * 4 + (t % 4 + 2 * ((t // 4) % 2)) % 4


def moved(x, pairs):
    return lax.ppermute(x, AXES, [(device_of(i), device_of(j)) for i, j in pairs])


def per_device(blocks, upper, arrow, tip, rhs, rhs_fixed):
    node_count = blocks.shape[1]
    effects = tip.shape[0]
    cols = 4
    count = lax.axis_size("tm") * cols
    col, shift = lax.axis_index("col"), 2 * (lax.axis_index("tm") % 2)
    pos = (col + shift) % cols
    t = lax.axis_index("tm") * cols + pos
    level_count = count.bit_length() - 1
    entries = []
    for s in [1 << k for k in range(level_count)]:
        entries += [(t + 1) % (2 * s) == s, (t + 1) // (2 * s) % 2]
    entries += [t == count - 1, 0, pos, t > 0]
    table = jnp.stack([jnp.asarray(v).astype(jnp.int32) for v in entries])
    sent = jnp.concatenate([blocks, arrow], axis=1)
    sent = jnp.where(shift > 0, jnp.concatenate([sent[2:4], sent[0:2]], axis=0), sent)
    got = lax.all_to_all(sent, "col", split_axis=0, concat_axis=0, tiled=True)
    pairs = upper.reshape(2, 2, node_count, TILE)
    pairs = jnp.where(shift > 0, pairs[::-1], pairs)
    wanted = jnp.concatenate([pairs[:, None], jnp.zeros_like(pairs)[:, None]], axis=1)
    wanted = wanted.reshape(4, 2, node_count, TILE)
    got, wanted = lax.optimization_barrier((got, wanted))
    wanted = lax.all_to_all(wanted, "col", split_axis=0, concat_axis=0, tiled=True)
    big, thin = shape(NODES, NODES), shape(NODES, TILE)
    state_shape, coupled = shape(SQUARE + EDGE, TILE), shape(WHOLE + EDGE, TILE)
    ma, mb, u, logs, q = call(
        lambda *refs: factor_first_kernel(2 * level_count + 2, *refs),
        0,
        (table, got, rhs),
        FACTORS + (state_shape,),
        WORK,
        flops=4 * 10**9,
    )
    low, high = call(
        lambda *refs: couple_first_kernel(2 * level_count + 2, *refs),
        0,
        (table, wanted),
        (coupled, coupled),
        flops=10**6,
    )
    middle, upper_middle = count // 2 - 1, 3 * count // 4 - 1
    top_pairs = [(middle, upper_middle), (count - 1, middle), (upper_middle, count - 1)]
    kept, late, sent_late = [], (), []
    level = 0
    while (1 << level) < count:
        s = 1 << level
        leaving = [(2 * k + 1) * s - 1 for k in range(count // (2 * s))]
        even, uneven = leaving[0::2], leaving[1::2]
        base = 2 * level
        last = 2 * s == count
        wn, near = call(
            near_kernel,
            base,
            (table, ma, mb, u, low, high),
            (big, shape(SQUARE, TILE)),
            flops=3 * 10**9,
        )
        if sent_late:
            near, far = lax.optimization_barrier((near, far))
            late = tuple(moved(far, pairs) for pairs in sent_late)
        arrived = [moved(near, [(i, i + s) for i in even])]
        if last:
            wf = jnp.zeros((NODES, NODES), F32)
            ws, edge = call(
                last_kernel,
                base,
                (table, ma, mb, u, logs, low, high, wn, q),
                (thin, shape(EDGE, TILE)),
                flops=10**9,
            )
            edge, arrived = lax.optimization_barrier((edge, arrived))
            edge = moved(edge, [(i, i + s) for i in even])
            parts = (q, *arrived, *late)
        else:
            arrived.append(moved(near, [(i, i - s) for i in uneven]))
            n = len(late)
            wf, ws, new, far, *q_adjusted = call(
                lambda flags, *refs: far_kernel(n, flags, *refs),
                base,
                (table, ma, mb, u, logs, low, high, wn, q, *late),
                (big, thin, coupled, state_shape) + (state_shape,) * (1 if n else 0),
                flops=4 * 10**9,
            )
            q = q_adjusted[0] if n else q
            new, arrived = lax.optimization_barrier((new, arrived))
            parts = (q, *arrived)
            sent_late = [top_pairs if 4 * s == count else [(i, i + s) for i in uneven]]
            if any(i >= s for i in even):
                sent_late.append([(i, i - s) for i in even if i >= s])
            low = moved(new, [(i, i + s) for i in even])
            high = moved(new, [(i, i - s) for i in uneven])
        kept.append((base, s, (ma, mb, u, wn, wf, ws)))
        n_parts = len(parts)
        ma, mb, u, logs = call(
            lambda *refs: factor_next_kernel(n_parts, *refs),
            base + 2,
            (table, *parts),
            FACTORS,
            WORK,
            flops=4 * 10**9,
        )
        level += 1
    whole_tip = jnp.eye(TILE, dtype=F32).at[0:effects, 0:effects].set(tip)
    whole_fixed = jnp.pad(rhs_fixed, (0, TILE - effects)).reshape(1, TILE)
    total = float(count * node_count + effects)
    n_late = len(late)
    (state,) = call(
        lambda *refs: root_kernel(total, n_late, *refs),
        2 * level_count,
        (table, ma, mb, u, logs, whole_tip, whole_fixed, edge, q, *late),
        (shape(1, NODES + TILE),),
        ((NODES, TILE), (TILE, TILE)),
        flops=10**8,
    )
    for base, s, factors in reversed(kept):
        leaving = [(2 * k + 1) * s - 1 for k in range(count // (2 * s))]
        if 2 * s < count:
            pairs = [(i - s, i) for i in leaving if i >= s]
            from_left = moved(state, top_pairs if 4 * s == count else pairs)
            from_right = moved(state, [(i + s, i) for i in leaving])
        else:
            from_left = jnp.zeros_like(state)
            from_right = moved(state, top_pairs)
        (state,) = call(
            back_kernel,
            base,
            (table, from_left, from_right, state) + factors,
            (shape(1, NODES + TILE),),
            flops=10**7,
        )
    rows = lax.all_to_all(state[:, 0:NODES], "col", split_axis=1, concat_axis=0, tiled=True)
    rows = jnp.where(shift > 0, jnp.roll(rows, 2, axis=0), rows)
    return (rows, state[0, NODES : NODES + effects], state[0, NODES + 64])


def solution(mesh):
    placed = (
        P("tm", None, "col"),
        P("tm", None, "col"),
        P("tm", None, "col"),
        P(),
        P("tm", None),
        P(),
    )
    return jax.shard_map(
        per_device,
        mesh=mesh,
        in_specs=placed,
        out_specs=(P("tm", "col"), P(), P()),
        check_vma=False,
    )
```
